32 devices in a mesh: view: 4 (over y, x), tile: 8 (over z, core).
Axes of the slice: x: 2, y: 2, z: 4, core: 2. Of those that a mesh axis runs over, the one named last changes fastest.
Arguments:
- object_band: float32 [8, 2, 512, 128], P('view', None, 'tile'), may hold values from -6 to 6
- dual_band: float32 [8, 2, 512, 128], P('view', None, 'tile'), may hold values from -6 to 6
- probe_field: float32 [2, 128, 128], replicated, may hold values from -6 to 6
- positions: int32 [8, 256], P('view', 'tile'), may hold values from 0 to 63
- live_counts: int32 [8, 8], P('view', 'tile'), may hold values from 1 to 32, 85 in all within a row
- photon_counts: int32 [8, 256, 128, 128], P('view', 'tile'), may hold values from 0 to 1023
- footprints: int32 [8, 8], P('view', 'tile'), may hold values from 0 to 6
- weights: bfloat16 [8, 128, 65536], P('view', None, 'tile'), may hold values from -0.046875 to 0.046875
- volume: float32 [2, 512, 128, 128], P(None, 'tile'), may hold values from -6 to 6
Outputs:
- object_new: float32 [8, 2, 512, 128], P('view', None, 'tile')
- dual_new: float32 [8, 2, 512, 128], P('view', None, 'tile')
- volume_new: float32 [2, 512, 128, 128], P(None, 'tile')
The draws below stay inside these ranges and needn't reach their ends.
Inputs may be any that keep to these rules, and one draw needn't show every extreme that they name: `positions`: offset of a slot's scan position from the first column of the tile that owns the slot. `live_counts`: the first that many of a tile's 32 slots are live; each view has exactly 85 live slots, and in each view some tile has all 32 live. `footprints`: first of the 2 consecutive detector tiles that a volume tile's shadow covers in a view.
All inputs are finite; a program needn't handle non-finite values. No bound on the sum of `live_counts` on one device may be relied on, other than what follows from the above.
Results may differ from the reference program's by a relative error of at most 0.006.
Values may be sent and summed in bfloat16 or wider, within the bound.
No kernel may reach another device: no remote copies, remote signals or barrier semaphores. Data moves between devices by JAX's collectives and lax.ppermute only.
A program may use at most 128 MiB of HBM per device.

```python
import math
import jax
import jax.numpy as jnp
import numpy as np
from jax import lax

PW = 128
PH = 128
CAP = 32
NY = 128
FOOT = 2
WT = 64
W = 512
VIEWS = 8
PATCHES = 85
VOX = 8192
FOOT_COLS = 128
N_TILE = 8


def plant(drawn, stream_key, least, top_value):
    longest = drawn.shape.index(max(drawn.shape))
    spots = []
    for shift in (0, 1):
        where = [jax.random.randint(jax.random.fold_in(stream_key, axis), (), 0, length) for axis, length in enumerate(drawn.shape)]
        where[longest] = (where[longest] + shift) % drawn.shape[longest]
        spots.append(tuple(where))
    return drawn.at[spots[0]].set(least).at[spots[1]].set(top_value)


def levels(stream_key, dims, pieces, low, largest):
    def one(dim, blocks):
        heights = jax.random.uniform(jax.random.fold_in(jax.random.fold_in(stream_key, 6), dim), (blocks,), jnp.float32, low / len(pieces), largest / len(pieces))
        return jnp.repeat(jnp.exp(heights), dims[dim] // blocks).reshape((-1,) + (1,) * (len(dims) - dim - 1))

    level = one(*pieces[0])
    for cut in pieces[1:]:
        level = level * one(*cut)
    return level


def split_up(number_of, total, most, skew):
    loads = [(1 << 20) // math.isqrt(rank ** skew) + 1 for rank in range(2, number_of + 1)]
    spare, holding = total - most - (number_of - 1), [1] * (number_of - 1)
    while spare > 0:
        movable = [i for i in range(number_of - 1) if holding[i] < most]
        mass, remaining = sum([loads[i] for i in movable]), spare
        for i in movable:
            addition = min(most - holding[i], max(1, remaining * loads[i] // mass), spare)
            holding[i] = holding[i] + addition
            spare = spare - addition
    return np.array([most] + holding)


def uneven(key, number_of, total, bound, slope):
    if number_of == 2:
        one = jax.random.randint(key, (), max(1, total - bound), min(bound, total - 1) + 1)
        return jnp.stack([one, total - one])
    lengths = jnp.asarray(split_up(number_of, total, bound, slope), jnp.int32)
    twos = (number_of - 1) // 2
    donor, receiver = lengths[1:1 + 2 * twos:2], lengths[2:2 + 2 * twos:2]
    slack = jnp.minimum(donor - 1, bound - receiver)
    shifted = jax.random.randint(jax.random.fold_in(key, 1), (twos,), 0, 1 << 20) % (slack + 1)
    lengths = lengths.at[1:1 + 2 * twos:2].set(donor - shifted).at[2:2 + 2 * twos:2].set(receiver + shifted)
    return lengths[jax.random.permutation(jax.random.fold_in(key, 2), number_of)]


def bell_draw(key, dims, width, most, pieces=(), kind=jnp.bfloat16):
    values = width * jax.random.normal(key, dims, jnp.float32)
    if pieces:
        values = values * levels(key, dims, pieces, -0.22, 0.18)
    return jnp.clip(values, -most, most).astype(kind)


def setup_inputs(seed: int = 0) -> dict:
    seeds = jax.random.split(jax.random.key(seed), 10)
    object_band = bell_draw(seeds[0], (VIEWS, 2, W, PH), 1.0, 6.0, ((0, 4), (2, 8)), jnp.float32)
    dual_band = bell_draw(seeds[1], (VIEWS, 2, W, PH), 1.0, 6.0, ((0, 4), (2, 8)), jnp.float32)
    probe_field = bell_draw(seeds[2], (2, PW, PH), 1.0, 6.0, (), jnp.float32)
    positions = plant(jax.random.randint(seeds[3], (VIEWS, N_TILE * CAP), 0, WT), jax.random.fold_in(seeds[3], 1), 0, WT - 1).astype(jnp.int32)
    live_counts = jax.vmap(lambda own: uneven(own, N_TILE, PATCHES, CAP, 2))(jax.random.split(seeds[4], VIEWS)).reshape((VIEWS, N_TILE)).astype(jnp.int32)
    photon_counts = plant(jax.random.randint(seeds[5], (VIEWS, N_TILE * CAP, PW, PH), 0, 1024), jax.random.fold_in(seeds[5], 1), 0, 1023).astype(jnp.int32)
    footprints = plant(jax.random.randint(seeds[6], (VIEWS, N_TILE), 0, N_TILE - FOOT + 1), jax.random.fold_in(seeds[6], 1), 0, N_TILE - FOOT).astype(jnp.int32)
    weights = bell_draw(seeds[7], (VIEWS, FOOT_COLS, W * NY), (FOOT * VOX) ** -0.5, 0.046875, ((0, 4), (2, 8)))
    volume = bell_draw(seeds[8], (2, W, NY, PH), 1.0, 6.0, ((1, 8),), jnp.float32)
    return dict(object_band=object_band, dual_band=dual_band, probe_field=probe_field, positions=positions, live_counts=live_counts, photon_counts=photon_counts, footprints=footprints, weights=weights, volume=volume)


rho_weight = 0.5
step_size = 0.5
prior_weight = 0.5
floor_term = 0.25

def tables(order_n):
    counter = jnp.arange(order_n, dtype=jnp.int32)
    phase_index = counter[:, None] * counter[None, :] % order_n
    angles = phase_index.astype(jnp.float32) * (2.0 * jnp.pi / order_n)
    scaling = 1.0 / jnp.sqrt(jnp.float32(order_n))
    return (jnp.cos(angles) * scaling, -jnp.sin(angles) * scaling)

def block_minus(parts):
    upper_half = jnp.concatenate([parts[0], -parts[1]], axis=1)
    lower_half = jnp.concatenate([parts[1], parts[0]], axis=1)
    return jnp.concatenate([upper_half, lower_half], axis=0).astype(jnp.bfloat16)

def block_plus(parts):
    upper_half = jnp.concatenate([parts[0], parts[1]], axis=1)
    lower_half = jnp.concatenate([-parts[1], parts[0]], axis=1)
    return jnp.concatenate([upper_half, lower_half], axis=0).astype(jnp.bfloat16)

def markov(padded):
    centre = padded[:, 1:-1, 1:-1, 1:-1]
    summed = jnp.zeros_like(centre)
    neighbours = (padded[:, 2:, 1:-1, 1:-1], padded[:, :-2, 1:-1, 1:-1], padded[:, 1:-1, 2:, 1:-1], padded[:, 1:-1, :-2, 1:-1], padded[:, 1:-1, 1:-1, 2:], padded[:, 1:-1, 1:-1, :-2])
    for neighbour in neighbours:
        difference = centre - neighbour
        summed = summed + difference / jnp.sqrt(1.0 + difference * difference)
    return summed

def patch_update(window, probe_field, counts_grid, dft_blocks):
    left_a, right_b, right_a, left_b = dft_blocks
    probe_re = probe_field[0]
    probe_im = probe_field[1]
    obj_re = window[0]
    obj_im = window[1]
    exit_wave = jnp.stack([probe_re * obj_re - probe_im * obj_im, probe_re * obj_im + probe_im * obj_re]).astype(jnp.bfloat16)
    num_cols = exit_wave.shape[1]
    num_rows = exit_wave.shape[2]
    columns_done = jnp.dot(left_a, exit_wave.reshape(2 * num_cols, num_rows), preferred_element_type=jnp.float32).astype(jnp.bfloat16)
    columns_done = columns_done.reshape(2, num_cols, num_rows).transpose(1, 0, 2).reshape(num_cols, 2 * num_rows)
    spectrum = jnp.dot(columns_done, right_b, preferred_element_type=jnp.float32)
    amplitude = jnp.sqrt(counts_grid.astype(jnp.float32)) / 16.0
    spec_re = spectrum[:, :num_rows]
    spec_im = spectrum[:, num_rows:]
    factor = amplitude / jnp.sqrt(spec_re * spec_re + spec_im * spec_im + floor_term)
    replaced = (spectrum * jnp.concatenate([factor, factor], axis=1)).astype(jnp.bfloat16)
    inverse_rows = jnp.dot(replaced, right_a, preferred_element_type=jnp.float32).astype(jnp.bfloat16)
    inverse_rows = inverse_rows.reshape(num_cols, 2, num_rows).transpose(1, 0, 2).reshape(2 * num_cols, num_rows)
    new_wave = jnp.dot(left_b, inverse_rows, preferred_element_type=jnp.float32).reshape(2, num_cols, num_rows)
    difference = new_wave - exit_wave.astype(jnp.float32)
    diff_re = difference[0]
    diff_im = difference[1]
    return jnp.stack([probe_re * diff_re + probe_im * diff_im, probe_re * diff_im - probe_im * diff_re, probe_re * probe_re + probe_im * probe_im])

def reference(object_band, dual_band, probe_field, positions, live_counts, photon_counts, footprints, weights, volume):
    dft_blocks = (block_minus(tables(PW)), block_plus(tables(PH)), block_minus(tables(PH)), block_plus(tables(PW)))
    volume_low = volume.astype(jnp.bfloat16).reshape(2, N_TILE, VOX, PH).transpose(1, 2, 0, 3).reshape(N_TILE, VOX, 2 * PH)

    def project_view(entries):
        view_weights, view_foot = entries

        def add_tile(summed, tile_index):
            weight_block = lax.dynamic_slice_in_dim(view_weights, tile_index * VOX, VOX, 1)
            window = jnp.dot(weight_block, volume_low[tile_index], preferred_element_type=jnp.float32)
            window = window.reshape(FOOT_COLS, 2, PH).transpose(1, 0, 2)
            first_col = (view_foot[tile_index] * WT).astype(jnp.int32)
            previous = lax.dynamic_slice_in_dim(summed, first_col, FOOT_COLS, 1)
            return (lax.dynamic_update_slice_in_dim(summed, previous + window, first_col, 1), None)
        summed, _ = lax.scan(add_tile, jnp.zeros((2, W, PH), jnp.float32), jnp.arange(N_TILE, dtype=jnp.int32))
        return summed
    projection = lax.map(project_view, (weights, footprints))

    def view_update(entries):
        obj_view, offsets, view_counts, view_photons = entries
        padded = jnp.pad(obj_view, ((0, 0), (0, 2 * WT), (0, 0)))
        accumulated = jnp.zeros((3, W + 2 * WT, PH), jnp.float32)

        def slot_step(carried, slot_entries):
            slot_index, offset_col, counts_grid = slot_entries
            tile_index = slot_index // CAP
            first_col = (tile_index * WT + offset_col).astype(jnp.int32)
            is_live = slot_index % CAP < view_counts[tile_index]

            def apply_patch(current):
                window = lax.dynamic_slice_in_dim(padded, first_col, PW, 1)
                contrib = patch_update(window, probe_field, counts_grid, dft_blocks)
                previous = lax.dynamic_slice_in_dim(current, first_col, PW, 1)
                return lax.dynamic_update_slice_in_dim(current, previous + contrib, first_col, 1)
            return (lax.cond(is_live, apply_patch, lambda current: current, carried), None)
        slot_indices = jnp.arange(N_TILE * CAP, dtype=jnp.int32)
        accumulated, _ = lax.scan(slot_step, accumulated, (slot_indices, offsets, view_photons))
        return accumulated[:, :W]
    update = lax.map(view_update, (object_band, positions, live_counts, photon_counts))
    object_new = object_band + update[:, 0:2] / (1.0 + update[:, 2:3]) - rho_weight * (object_band - projection - dual_band)
    dual_new = dual_band + projection - object_new
    residual = (projection - object_new + dual_band).astype(jnp.bfloat16)

    def back_tile(tile_index):
        weight_block = lax.dynamic_slice_in_dim(weights, tile_index * VOX, VOX, 2).astype(jnp.float32)
        starts = (footprints[:, tile_index] * WT).astype(jnp.int32)
        windows = jax.vmap(lambda resid_view, first_col: lax.dynamic_slice_in_dim(resid_view, first_col, FOOT_COLS, 1))(residual, starts)
        return jnp.einsum('acx,akch->kxh', weight_block, windows.astype(jnp.float32))
    gradient = lax.map(back_tile, jnp.arange(N_TILE, dtype=jnp.int32))
    gradient = gradient.transpose(1, 0, 2, 3).reshape(2, W, NY, PH)
    half_step = volume - step_size * gradient
    padded_volume = jnp.pad(half_step, ((0, 0), (1, 1), (1, 1), (1, 1)))
    volume_new = half_step - step_size * prior_weight * markov(padded_volume)
    return (object_new, dual_new, volume_new)
```

```python
import functools
import numpy as np
import jax
import jax.numpy as jnp
from jax import lax
from jax.experimental import pallas as pl
from jax.experimental.pallas import tpu as pltpu
from jax.sharding import PartitionSpec as P

rho_weight = 0.5
step_size = 0.5
prior_weight = 0.5
floor_term = 0.25

F32 = jnp.float32
BF16 = jnp.bfloat16
VMEM = pltpu.VMEM
SMEM = pltpu.SMEM


def passed_along(value, axis, steps):
    count = lax.axis_size(axis)
    initial, last = (max(0, -steps), min(count, count - steps))
    return lax.ppermute(value, axis, [(source, source + steps) for source in range(initial, last)])


def swapped(value, axis, mask):
    count = lax.axis_size(axis)
    return lax.ppermute(value, axis, [(i, i ^ mask) for i in range(count)])


def masks_of(count):
    return [1 << b for b in range(count.bit_length() - 1)]


def packed_rank(value, masks):
    rank = jnp.zeros_like(value)
    for place, mask in enumerate(masks):
        rank = rank + jnp.where((value & mask) != 0, 1 << place, 0)
    return rank


def dft_block(order_n, inverse):
    counter = np.arange(order_n)
    angles = (counter[:, None] * counter[None, :] % order_n) * (2.0 * np.pi / order_n)
    re = np.cos(angles) / np.sqrt(order_n)
    im = -np.sin(angles) / np.sqrt(order_n)
    im = -im if inverse else im
    return jnp.asarray(np.block([[re, -im], [im, re]]).astype(np.float32)).astype(BF16)


def project_kernel(spots, weights_ref, volume_ref, placed_ref, total):
    step = pl.program_id(0)
    views, cols, span = weights_ref.shape
    rows = volume_ref.shape[3]

    @pl.when(step == 0)
    def _():
        total[...] = jnp.zeros_like(total)

    low = jnp.concatenate(
        [volume_ref[0].reshape(span, rows), volume_ref[1].reshape(span, rows)], axis=1
    ).astype(BF16)
    total[...] += jnp.dot(
        weights_ref[...].reshape(views * cols, span), low, preferred_element_type=F32
    )

    @pl.when(step == pl.num_programs(0) - 1)
    def _():
        placed_ref[...] = jnp.zeros_like(placed_ref)
        width = placed_ref.shape[3]
        for v in range(views):
            for part in range(cols // width):
                spot = spots[v, part]
                first = v * cols + part * width
                for k in range(2):
                    placed_ref[spot, v, k] = total[
                        first : first + width, k * rows : (k + 1) * rows
                    ].astype(BF16)


def project(spots, weights, volume, tiles, tile_cols):
    views, cols, voxels = weights.shape
    _, vcols, depth, rows = volume.shape
    chunk = max(1, vcols // 8)
    span = chunk * depth
    return pl.pallas_call(
        project_kernel,
        out_shape=jax.ShapeDtypeStruct((tiles, views, 2, tile_cols, rows), BF16),
        grid_spec=pltpu.PrefetchScalarGridSpec(
            num_scalar_prefetch=1,
            grid=(vcols // chunk,),
            in_specs=[
                pl.BlockSpec((views, cols, span), lambda i, s: (0, 0, i)),
                pl.BlockSpec((2, chunk, depth, rows), lambda i, s: (0, i, 0, 0)),
            ],
            out_specs=pl.BlockSpec((tiles, views, 2, tile_cols, rows), lambda i, s: (0,) * 5),
            scratch_shapes=[VMEM((views * cols, 2 * rows), F32)],
        ),
        cost_estimate=pl.CostEstimate(
            flops=4 * views * cols * voxels * rows,
            transcendentals=0,
            bytes_accessed=weights.size * 2 + volume.size * 4,
        ),
        name="project",
    )(spots, weights, volume)


GROUP = 4


def patch_kernel(
    positions,
    live,
    own_ref,
    one_ref,
    two_ref,
    probe_ref,
    forward_ref,
    inverse_ref,
    counts_ref,
    near_ref,
    ahead_ref,
    reach,
    total,
    buffer,
    sems,
):
    views, _, width, rows = own_ref.shape
    cols = probe_ref.shape[1]
    span = 3 * width
    for part, ref in enumerate((own_ref, one_ref, two_ref)):
        reach[:, :, part * width : (part + 1) * width, :] = ref[...]
    total[...] = jnp.zeros_like(total)
    starts = [0]
    for v in range(views):
        starts.append(starts[-1] + lax.div(live[v] + (GROUP - 1), GROUP))

    def located(step):
        view, first = 0, 0
        for v in range(1, views):
            after = (step >= starts[v]).astype(jnp.int32)
            view = view + after
            first = jnp.where(after == 1, starts[v], first)
        return view, (step - first) * GROUP

    def fetch(step, slot):
        view, first = located(step)
        return pltpu.make_async_copy(
            counts_ref.at[view, pl.ds(first, GROUP)], buffer.at[slot], sems.at[slot]
        )

    fetch(0, 0).start()

    def body(step, carry):
        slot = step & 1
        view, first = located(step)
        pltpu.make_async_copy(
            counts_ref.at[view, pl.ds(first, GROUP)], buffer.at[slot], sems.at[slot]
        ).wait()

        @pl.when(step + 1 < starts[views])
        def _():
            fetch(step + 1, 1 - slot).start()

        probe_re = probe_ref[0]
        probe_im = probe_ref[1]
        spots = []
        exits = []
        for g in range(GROUP):
            offset = positions[view, first + g]
            spots.append(jnp.where(first + g < live[view], offset, span))
            obj_re = reach[view, 0, pl.ds(offset, cols), :]
            obj_im = reach[view, 1, pl.ds(offset, cols), :]
            wave_re = (probe_re * obj_re - probe_im * obj_im).astype(BF16)
            wave_im = (probe_re * obj_im + probe_im * obj_re).astype(BF16)
            exits.append(jnp.concatenate([wave_re, wave_im], axis=0))
        waves = jnp.concatenate(exits, axis=1)
        done = jnp.dot(forward_ref[...], waves, preferred_element_type=F32).astype(BF16)
        done = jnp.concatenate(
            [
                jnp.concatenate(
                    [
                        done[:cols, g * rows : (g + 1) * rows],
                        done[cols:, g * rows : (g + 1) * rows],
                    ],
                    axis=1,
                )
                for g in range(GROUP)
            ],
            axis=0,
        )
        spectrum = jnp.dot(done, inverse_ref[...], preferred_element_type=F32)
        spec_re = spectrum[:, :rows]
        spec_im = spectrum[:, rows:]
        counts = buffer[slot].reshape(GROUP * cols, rows).astype(F32)
        square = spec_re * spec_re + spec_im * spec_im + floor_term
        factor = (counts * (1.0 / 16.0)) * lax.rsqrt(jnp.maximum(counts * square, 1e-6))
        replaced = jnp.concatenate(
            [(spec_re * factor).astype(BF16), (spec_im * factor).astype(BF16)], axis=1
        )
        back = jnp.dot(replaced, forward_ref[...], preferred_element_type=F32).astype(BF16)
        back = jnp.concatenate(
            [
                jnp.concatenate(
                    [
                        back[g * cols : (g + 1) * cols, :rows],
                        back[g * cols : (g + 1) * cols, rows:],
                    ],
                    axis=0,
                )
                for g in range(GROUP)
            ],
            axis=1,
        )
        wave = jnp.dot(inverse_ref[...], back, preferred_element_type=F32)
        power = probe_re * probe_re + probe_im * probe_im
        for g in range(GROUP):
            diff = wave[:, g * rows : (g + 1) * rows] - exits[g].astype(F32)
            diff_re = diff[:cols]
            diff_im = diff[cols:]
            place = pl.ds(spots[g], cols)
            total[view, 0, place, :] += probe_re * diff_re + probe_im * diff_im
            total[view, 1, place, :] += probe_re * diff_im - probe_im * diff_re
            total[view, 2, place, :] += power
        return carry

    lax.fori_loop(0, starts[views], body, 0)
    near_ref[...] = total[:, :, :width, :]
    for part in range(2):
        ahead_ref[part] = total[:, :, (part + 1) * width : (part + 2) * width, :].astype(BF16)


def patches(positions, live, own, one, two, probe, forward, inverse, counts):
    views, _, width, rows = own.shape
    cols = probe.shape[1]
    slots = counts.shape[1]
    vmem = pl.BlockSpec(memory_space=VMEM)
    smem = pl.BlockSpec(memory_space=SMEM)
    return pl.pallas_call(
        patch_kernel,
        out_shape=(
            jax.ShapeDtypeStruct((views, 3, width, rows), F32),
            jax.ShapeDtypeStruct((2, views, 3, width, rows), BF16),
        ),
        in_specs=[smem, smem] + [vmem] * 6 + [pl.BlockSpec(memory_space=pl.ANY)],
        out_specs=(vmem, vmem),
        scratch_shapes=[
            VMEM((views, 2, 3 * width, rows), F32),
            VMEM((views, 3, 3 * width + cols, rows), F32),
            VMEM((2, GROUP, cols, rows), jnp.int32),
            pltpu.SemaphoreType.DMA((2,)),
        ],
        cost_estimate=pl.CostEstimate(
            flops=views * slots * 16 * cols * cols * rows,
            transcendentals=0,
            bytes_accessed=counts.size * 4,
        ),
        name="patches",
    )(positions, live, own, one, two, probe, forward, inverse, counts)


def cut_kernel(spots, *refs):
    pieces, windows_ref, held = refs[:-2], refs[-2], refs[-1]
    first = 0
    for ref in pieces:
        held[first : first + ref.shape[0]] = ref[...]
        first += ref.shape[0]
    views, planes, cols, rows = windows_ref.shape
    width = held.shape[3]
    for v in range(views):
        for part in range(cols // width):
            for k in range(planes):
                windows_ref[v, k, part * width : (part + 1) * width] = held[spots[v, part], v, k]


def cut(spots, pieces, cols):
    blocks = sum(piece.shape[0] for piece in pieces)
    _, views, planes, width, rows = pieces[0].shape
    vmem = pl.BlockSpec(memory_space=VMEM)
    return pl.pallas_call(
        cut_kernel,
        out_shape=jax.ShapeDtypeStruct((views, planes, cols, rows), BF16),
        in_specs=[pl.BlockSpec(memory_space=SMEM)] + [vmem] * len(pieces),
        out_specs=vmem,
        scratch_shapes=[VMEM((blocks, views, planes, width, rows), BF16)],
        name="cut",
    )(spots, *pieces)


def half_kernel(groups, mine, *refs):
    weight_refs = refs[:groups]
    window_refs = refs[groups : 2 * groups]
    volume_ref, half_ref, low_ref, high_ref = refs[2 * groups :]
    step = pl.program_id(0)
    _, chunk, depth, rows = half_ref.shape
    gradient = None
    for weights, windows in zip(weight_refs, window_refs):
        for v in range(weights.shape[0]):
            both = jnp.concatenate([windows[v, 0], windows[v, 1]], axis=1)
            product = lax.dot_general(
                weights[v], both, (((0,), (0,)), ((), ())), preferred_element_type=F32
            )
            gradient = product if gradient is None else gradient + product
    for k in range(2):
        plane = gradient[:, k * rows : (k + 1) * rows].reshape(chunk, depth, rows)
        half_ref[k] = volume_ref[k] - step_size * plane

    @pl.when(step == 0)
    def _():
        low_ref[...] = half_ref[:, :1]

    @pl.when(step == pl.num_programs(0) - 1)
    def _():
        high_ref[...] = half_ref[:, chunk - 1 :]


def half_step_of(mine, weights, pieces, windows, volume):
    groups = len(windows)
    views, cols, voxels = weights.shape
    _, vcols, depth, rows = volume.shape
    share = vcols // groups
    chunk = min(4, share)
    span = chunk * depth
    steps = share // chunk
    edge = pl.BlockSpec((2, 1, depth, rows), lambda i, m: (0, 0, 0, 0))
    whole = pl.BlockSpec(windows[0].shape, lambda i, m: (0, 0, 0, 0))
    piece = pl.BlockSpec((views, cols, span), lambda i, m: (0, 0, i))
    return pl.pallas_call(
        functools.partial(half_kernel, groups),
        out_shape=(
            jax.ShapeDtypeStruct((2, share, depth, rows), F32),
            jax.ShapeDtypeStruct((2, 1, depth, rows), F32),
            jax.ShapeDtypeStruct((2, 1, depth, rows), F32),
        ),
        grid_spec=pltpu.PrefetchScalarGridSpec(
            num_scalar_prefetch=1,
            grid=(steps,),
            in_specs=[pl.BlockSpec((views, cols, span), lambda i, m: (0, 0, m[0] * steps + i))]
            + [piece] * (groups - 1)
            + [whole] * groups
            + [pl.BlockSpec((2, chunk, depth, rows), lambda i, m: (0, m[0] * steps + i, 0, 0))],
            out_specs=(
                pl.BlockSpec((2, chunk, depth, rows), lambda i, m: (0, i, 0, 0)),
                edge,
                edge,
            ),
        ),
        name="half_step",
    )(mine, weights, *pieces, *windows, volume)


def bent(d):
    return d * lax.rsqrt(1.0 + d * d)


def prior_kernel(mine, half_ref, before_ref, after_ref, out_ref, first_ref, second_ref, link):
    step = pl.program_id(0)
    last = pl.num_programs(0) - 1
    depth, rows = half_ref.shape[2:]
    lane = lax.broadcasted_iota(jnp.int32, (depth, rows), 1)
    level = lax.broadcasted_iota(jnp.int32, (depth, rows), 0)
    for k, low_ref in ((0, first_ref), (1, second_ref)):
        here = half_ref[k, step]

        @pl.when(step == 0)
        def _():
            link[k] = bent(before_ref[k, 0] - here)

        following = half_ref[k, jnp.minimum(step + 1, last)]
        following = jnp.where(step == last, after_ref[k, 0], following)
        ahead = bent(here - following)
        prior = ahead - link[k]
        link[k] = ahead
        beyond = jnp.where(lane == rows - 1, 0.0, pltpu.roll(here, rows - 1, 1))
        pair = bent(here - beyond)
        alone = bent(here)
        prior = prior + pair - jnp.where(lane == 0, -alone, pltpu.roll(pair, 1, 1))
        beyond = jnp.where(level == depth - 1, 0.0, pltpu.roll(here, depth - 1, 0))
        pair = bent(here - beyond)
        prior = prior + pair - jnp.where(level == 0, -alone, pltpu.roll(pair, 1, 0))
        fresh = here - step_size * prior_weight * prior
        out_ref[k, 0] = fresh
        low_ref[...] = fresh.astype(BF16)


def prior_step(mine, half, before, after, vcols):
    _, share, depth, rows = half.shape
    edge = pl.BlockSpec((2, 1, depth, rows), lambda i, m: (0, 0, 0, 0))
    low = pl.BlockSpec((depth, rows), lambda i, m: (i, 0))
    return pl.pallas_call(
        prior_kernel,
        out_shape=(
            jax.ShapeDtypeStruct((2, vcols, depth, rows), F32),
            jax.ShapeDtypeStruct((share * depth, rows), BF16),
            jax.ShapeDtypeStruct((share * depth, rows), BF16),
        ),
        grid_spec=pltpu.PrefetchScalarGridSpec(
            num_scalar_prefetch=1,
            grid=(share,),
            in_specs=[
                pl.BlockSpec((2, share, depth, rows), lambda i, m: (0, 0, 0, 0)),
                edge,
                edge,
            ],
            out_specs=(
                pl.BlockSpec((2, 1, depth, rows), lambda i, m: (0, m[0] * share + i, 0, 0)),
                low,
                low,
            ),
            scratch_shapes=[VMEM((2, depth, rows), F32)],
        ),
        name="prior",
    )(mine, half, before, after)


def place_kernel(where, piece_ref, whole_ref, out_ref):
    out_ref[...] = piece_ref[...].reshape(out_ref.shape).astype(F32)


def place(where, piece, whole, plane, groups):
    _, vcols, depth, rows = whole.shape
    share = vcols // groups
    chunk = max(1, share // 2)
    steps = share // chunk
    return pl.pallas_call(
        place_kernel,
        out_shape=jax.ShapeDtypeStruct(whole.shape, F32),
        grid_spec=pltpu.PrefetchScalarGridSpec(
            num_scalar_prefetch=1,
            grid=(steps,),
            in_specs=[
                pl.BlockSpec((chunk * depth, rows), lambda i, w: (i, 0)),
                pl.BlockSpec(memory_space=pl.ANY),
            ],
            out_specs=pl.BlockSpec(
                (1, chunk, depth, rows), lambda i, w: (plane, w[0] * steps + i, 0, 0)
            ),
        ),
        input_output_aliases={2: 0},
        name="place",
    )(where, piece, whole)


def per_device(
    object_band,
    dual_band,
    probe_field,
    positions,
    live_counts,
    photon_counts,
    footprints,
    weights,
    volume,
):
    tiles, groups = lax.axis_size("tile"), lax.axis_size("view")
    tile, group = lax.axis_index("tile"), lax.axis_index("view")
    tile_cols = object_band.shape[2]
    foot_cols = weights.shape[1]
    vcols = volume.shape[1]
    share_voxels = weights.shape[2] // groups
    tile_masks = masks_of(tiles)
    forward = dft_block(probe_field.shape[1], False)
    inverse = dft_block(probe_field.shape[1], True)
    mine = group.astype(jnp.int32).reshape(1)
    blocks = footprints + jnp.arange(foot_cols // tile_cols, dtype=jnp.int32)[None, :]
    relative = blocks ^ tile.astype(jnp.int32)

    ahead_one = passed_along(object_band, "tile", -1)
    ahead_two = passed_along(object_band, "tile", -2)
    weight_pieces = [
        swapped(
            lax.dynamic_slice_in_dim(weights, (group ^ j) * share_voxels, share_voxels, 2),
            "view",
            j,
        )
        for j in range(1, groups)
    ]

    placed = project(packed_rank(relative, tile_masks[::-1]), weights, volume, tiles, tile_cols)
    held = placed
    for mask in tile_masks:
        half = held.shape[0] // 2
        arrived = swapped(held[half:], "tile", mask)
        held = held[:half].astype(F32) + arrived.astype(F32)
        held = held.astype(BF16) if half > 1 else held
    projection = held[0]

    near, ahead = patches(
        positions,
        live_counts[:, 0],
        object_band,
        ahead_one,
        ahead_two,
        probe_field,
        forward,
        inverse,
        photon_counts,
    )
    from_one = passed_along(ahead[0], "tile", 1).astype(F32)
    from_two = passed_along(ahead[1], "tile", 2).astype(F32)
    summed = near + from_one + from_two
    object_new = (
        object_band
        + summed[:, 0:2] / (1.0 + summed[:, 2:3])
        - rho_weight * (object_band - projection - dual_band)
    )
    dual_new = dual_band + projection - object_new
    residual = (projection - object_new + dual_band).astype(BF16)

    pieces = [residual[None]]
    for mask in tile_masks[::-1]:
        gathered = pieces[0] if len(pieces) == 1 else jnp.concatenate(pieces, axis=0)
        pieces.append(swapped(gathered, "tile", mask))
    windows = cut(packed_rank(relative, tile_masks[::-1]), pieces, foot_cols)
    all_windows = [windows] + [swapped(windows, "view", j) for j in range(1, groups)]

    half, low_edge, high_edge = half_step_of(mine, weights, weight_pieces, all_windows, volume)
    order = [g * tiles + t for t in range(tiles) for g in range(groups)]
    up = list(zip(order[:-1], order[1:]))
    before = lax.ppermute(high_edge, ("view", "tile"), up)
    after = lax.ppermute(low_edge, ("view", "tile"), [(b, a) for a, b in up])
    volume_new, *shares = prior_step(mine, half, before, after, vcols)
    view_masks = masks_of(groups)
    for plane, masks in ((0, view_masks), (1, view_masks[::-1])):
        held = {0: shares[plane]}
        for mask in masks:
            held.update({j ^ mask: swapped(value, "view", mask) for j, value in held.items()})
        for j, value in held.items():
            if j:
                volume_new = place(mine ^ j, value, volume_new, plane, groups)
    return (object_new, dual_new, volume_new)


def solution(mesh):
    return jax.shard_map(
        per_device,
        mesh=mesh,
        in_specs=(
            P("view", None, "tile", None),
            P("view", None, "tile", None),
            P(),
            P("view", "tile"),
            P("view", "tile"),
            P("view", "tile", None, None),
            P("view", "tile"),
            P("view", None, "tile"),
            P(None, "tile", None, None),
        ),
        out_specs=(
            P("view", None, "tile", None),
            P("view", None, "tile", None),
            P(None, "tile", None, None),
        ),
        check_vma=False,
    )
```

```python
import functools
import numpy as np
import jax
import jax.numpy as jnp
from jax import lax
from jax.experimental import pallas as pl
from jax.experimental.pallas import tpu as pltpu
from jax.sharding import PartitionSpec as P


rho_weight = 0.5
step_size = 0.5
prior_weight = 0.5
floor_term = 0.25


F32 = jnp.float32
BF16 = jnp.bfloat16
VMEM = pltpu.VMEM
SMEM = pltpu.SMEM


def passed_along(value, axis, steps):
    count = lax.axis_size(axis)
    initial, last = (max(0, -steps), min(count, count - steps))
    return lax.ppermute(value, axis, [(source, source + steps) for source in range(initial, last)])


def near(*arrays):
    return tuple(pltpu.with_memory_space_constraint(array, VMEM) for array in arrays)


def limit(mebibytes):
    return pltpu.CompilerParams(vmem_limit_bytes=mebibytes << 20)


def swapped(value, axis, mask):
    count = lax.axis_size(axis)
    return lax.ppermute(value, axis, [(i, i ^ mask) for i in range(count)])


def masks_of(count):
    return [1 << b for b in range(count.bit_length() - 1)]


def dft_block(order_n, inverse):
    counter = np.arange(order_n)
    angles = (counter[:, None] * counter[None, :] % order_n) * (2.0 * np.pi / order_n)
    re = np.cos(angles) / np.sqrt(order_n)
    im = -np.sin(angles) / np.sqrt(order_n)
    im = -im if inverse else im
    return jnp.asarray(np.block([[re, -im], [im, re]]).astype(np.float32)).astype(BF16)


def deal_kernel(weights_ref, *refs):
    *shares, sems = refs
    group = lax.axis_index("view")
    copies = []
    for j, ref in list(enumerate(shares))[1:] + [(0, shares[0])]:
        size = ref.shape[2]
        first = pl.multiple_of((group ^ j) * size, size)
        copies.append(
            pltpu.make_async_copy(weights_ref.at[:, :, pl.ds(first, size)], ref, sems.at[j])
        )
        copies[-1].start()
    for copy in copies:
        copy.wait()


def deal(weights, groups):
    views, cols, voxels = weights.shape
    vmem = pl.BlockSpec(memory_space=VMEM)
    return pl.pallas_call(
        deal_kernel,
        out_shape=(VMEM((views, cols, voxels // groups), BF16),) * groups,
        in_specs=[pl.BlockSpec(memory_space=pl.ANY)],
        out_specs=(vmem,) * groups,
        scratch_shapes=[pltpu.SemaphoreType.DMA((groups,))],
        compiler_params=limit(8),
        name="deal",
    )(pltpu.with_memory_space_constraint(weights, pltpu.HBM))


def ranks(footprints, views, parts, tiles):
    tile = lax.axis_index("tile")
    found = []
    for v in range(views):
        row = []
        for part in range(parts):
            other = (footprints[v] + part) ^ tile
            row.append((other >> 1) + (other & 1) * (tiles // 2))
        found.append(row)
    return found


def project_kernel(footprints, volume_ref, *refs):
    *shares, keep_ref, send_ref, part_ref = refs
    views, cols, size = shares[0].shape
    _, count, _, rows = part_ref.shape
    half, _, _, width, _ = keep_ref.shape
    group = lax.axis_index("view")
    keep_ref[...] = jnp.zeros_like(keep_ref)
    send_ref[...] = jnp.zeros_like(send_ref)
    part_ref[...] = volume_ref[:, pl.ds(group * count, count)]
    total = jnp.zeros((views * cols, 2 * rows), F32)
    for j, ref in enumerate(shares):
        first = (group ^ j) * count
        low = jnp.concatenate(
            [volume_ref[k, pl.ds(first, count)].reshape(size, rows).astype(BF16) for k in range(2)],
            axis=1,
        )
        total = total + jnp.dot(
            ref[...].reshape(views * cols, size), low, preferred_element_type=F32
        )
    spots = ranks(footprints, views, cols // width, 2 * half)
    for v in range(views):
        for part in range(cols // width):
            first = v * cols + part * width
            spot = spots[v][part]
            for ref, wanted, index in (
                (keep_ref, spot < half, spot),
                (send_ref, spot >= half, spot - half),
            ):

                @pl.when(wanted)
                def _():
                    for k in range(2):
                        ref[index, v, k] = total[
                            first : first + width, k * rows : (k + 1) * rows
                        ].astype(BF16)


def project(footprints, shares, volume, tiles, tile_cols):
    groups = len(shares)
    views, _, _ = shares[0].shape
    _, vcols, depth, rows = volume.shape
    vmem = pl.BlockSpec(memory_space=VMEM)
    placed = VMEM((tiles // 2, views, 2, tile_cols, rows), BF16)
    return pl.pallas_call(
        project_kernel,
        out_shape=(placed, placed, VMEM((2, vcols // groups, depth, rows), F32)),
        in_specs=[pl.BlockSpec(memory_space=SMEM)] + [vmem] * (groups + 1),
        out_specs=(vmem,) * 3,
        compiler_params=limit(16),
        name="project",
    )(footprints, *near(volume, *shares))


def fold_kernel(keep_ref, arrived_ref, *refs):
    for n, ref in enumerate(refs):
        ref[...] = (keep_ref[n].astype(F32) + arrived_ref[n].astype(F32)).astype(ref.dtype)


def fold(keep, arrived):
    vmem = pl.BlockSpec(memory_space=VMEM)
    return pl.pallas_call(
        fold_kernel,
        out_shape=tuple(VMEM(keep.shape[1:], BF16 if n else F32) for n in range(keep.shape[0])),
        in_specs=[vmem] * 2,
        out_specs=(vmem,) * keep.shape[0],
        compiler_params=limit(8),
        name="fold",
    )(*near(keep, arrived))


GROUP = 4


def patch_kernel(
    positions,
    live,
    own_ref,
    one_ref,
    two_ref,
    probe_ref,
    forward_ref,
    inverse_ref,
    counts_ref,
    token_ref,
    near_ref,
    ahead_one_ref,
    ahead_two_ref,
    reach,
    total,
    buffer,
    sems,
):
    views, _, width, rows = own_ref.shape
    cols = probe_ref.shape[1]
    span = 3 * width
    for part, ref in enumerate((own_ref, one_ref, two_ref)):
        reach[:, :, part * width : (part + 1) * width, :] = ref[...]
    total[...] = jnp.zeros_like(total)
    starts = [0]
    for v in range(views):
        starts.append(starts[-1] + lax.div(live[v] + (GROUP - 1), GROUP))

    def located(step):
        view, first = 0, 0
        for v in range(1, views):
            after = (step >= starts[v]).astype(jnp.int32)
            view = view + after
            first = jnp.where(after == 1, starts[v], first)
        return view, (step - first) * GROUP

    def fetch(step, slot):
        view, first = located(step)
        return pltpu.make_async_copy(
            counts_ref.at[view, pl.ds(first, GROUP)], buffer.at[slot], sems.at[slot]
        )

    fetch(0, 0).start()

    def body(step, carry):
        slot = step & 1
        view, first = located(step)
        pltpu.make_async_copy(
            counts_ref.at[view, pl.ds(first, GROUP)], buffer.at[slot], sems.at[slot]
        ).wait()

        @pl.when(step + 1 < starts[views])
        def _():
            fetch(step + 1, 1 - slot).start()

        probe_re = probe_ref[0]
        probe_im = probe_ref[1]
        spots = []
        exits = []
        for g in range(GROUP):
            offset = positions[view, first + g]
            spots.append(jnp.where(first + g < live[view], offset, span))
            obj_re = reach[view, 0, pl.ds(offset, cols), :]
            obj_im = reach[view, 1, pl.ds(offset, cols), :]
            wave_re = (probe_re * obj_re - probe_im * obj_im).astype(BF16)
            wave_im = (probe_re * obj_im + probe_im * obj_re).astype(BF16)
            exits.append(jnp.concatenate([wave_re, wave_im], axis=0))
        waves = jnp.concatenate(exits, axis=1)
        done = jnp.dot(forward_ref[...], waves, preferred_element_type=F32).astype(BF16)
        done = jnp.concatenate(
            [
                jnp.concatenate(
                    [
                        done[:cols, g * rows : (g + 1) * rows],
                        done[cols:, g * rows : (g + 1) * rows],
                    ],
                    axis=1,
                )
                for g in range(GROUP)
            ],
            axis=0,
        )
        spectrum = jnp.dot(done, inverse_ref[...], preferred_element_type=F32)
        spec_re = spectrum[:, :rows]
        spec_im = spectrum[:, rows:]
        counts = buffer[slot].reshape(GROUP * cols, rows).astype(F32)
        square = spec_re * spec_re + spec_im * spec_im + floor_term
        factor = (counts * (1.0 / 16.0)) * lax.rsqrt(jnp.maximum(counts * square, 1e-6))
        replaced = jnp.concatenate(
            [(spec_re * factor).astype(BF16), (spec_im * factor).astype(BF16)], axis=1
        )
        back = jnp.dot(replaced, forward_ref[...], preferred_element_type=F32).astype(BF16)
        back = jnp.concatenate(
            [
                jnp.concatenate(
                    [
                        back[g * cols : (g + 1) * cols, :rows],
                        back[g * cols : (g + 1) * cols, rows:],
                    ],
                    axis=0,
                )
                for g in range(GROUP)
            ],
            axis=1,
        )
        wave = jnp.dot(inverse_ref[...], back, preferred_element_type=F32)
        power = probe_re * probe_re + probe_im * probe_im
        for g in range(GROUP):
            diff = wave[:, g * rows : (g + 1) * rows] - exits[g].astype(F32)
            diff_re = diff[:cols]
            diff_im = diff[cols:]
            place = pl.ds(spots[g], cols)
            total[view, 0, place, :] += probe_re * diff_re + probe_im * diff_im
            total[view, 1, place, :] += probe_re * diff_im - probe_im * diff_re
            total[view, 2, place, :] += power
        return carry

    lax.fori_loop(0, starts[views], body, 0)
    near_ref[...] = total[:, :, :width, :]
    for part, ref in ((1, ahead_one_ref), (2, ahead_two_ref)):
        ref[...] = total[:, :, part * width : (part + 1) * width, :].astype(BF16)


def patches(positions, live, own, one, two, probe, forward, inverse, counts, token):
    views, _, width, rows = own.shape
    cols = probe.shape[1]
    slots = counts.shape[1]
    vmem = pl.BlockSpec(memory_space=VMEM)
    smem = pl.BlockSpec(memory_space=SMEM)
    return pl.pallas_call(
        patch_kernel,
        out_shape=(
            VMEM((views, 3, width, rows), F32),
            VMEM((views, 3, width, rows), BF16),
            VMEM((views, 3, width, rows), BF16),
        ),
        in_specs=[smem, smem] + [vmem] * 6 + [pl.BlockSpec(memory_space=pl.ANY)] * 2,
        out_specs=(vmem, vmem, vmem),
        scratch_shapes=[
            VMEM((views, 2, 3 * width, rows), F32),
            VMEM((views, 3, 3 * width + cols, rows), F32),
            VMEM((2, GROUP, cols, rows), jnp.int32),
            pltpu.SemaphoreType.DMA((2,)),
        ],
        compiler_params=limit(20),
        cost_estimate=pl.CostEstimate(
            flops=views * slots * 16 * cols * cols * rows,
            transcendentals=0,
            bytes_accessed=counts.size * 4,
        ),
        name="patches",
    )(positions, live, own, *near(one, two), probe, forward, inverse, counts, *near(token))


def cut_kernel(tiles, footprints, *refs):
    pieces, windows_ref = refs[:-1], refs[-1]
    views, _, cols, _ = windows_ref.shape
    width = pieces[0].shape[3]
    spots = ranks(footprints, views, cols // width, tiles)
    for v in range(views):
        for part in range(cols // width):
            first = 0
            for ref in pieces:
                inside = spots[v][part] - first

                @pl.when((inside >= 0) & (inside < ref.shape[0]))
                def _():
                    windows_ref[v, :, part * width : (part + 1) * width] = ref[inside, v]

                first += ref.shape[0]


def cut(footprints, pieces, cols, tiles):
    _, views, planes, _, rows = pieces[0].shape
    vmem = pl.BlockSpec(memory_space=VMEM)
    return pl.pallas_call(
        functools.partial(cut_kernel, tiles),
        out_shape=VMEM((views, planes, cols, rows), BF16),
        in_specs=[pl.BlockSpec(memory_space=SMEM)] + [vmem] * len(pieces),
        out_specs=vmem,
        compiler_params=limit(8),
        name="cut",
    )(footprints, *near(*pieces))


def bent(d):
    return d * lax.rsqrt(1.0 + d * d)


def settled(here, behind, ahead):
    depth, rows = here.shape
    lane = lax.broadcasted_iota(jnp.int32, (depth, rows), 1)
    level = lax.broadcasted_iota(jnp.int32, (depth, rows), 0)
    prior = ahead - behind
    beyond = jnp.where(lane == rows - 1, 0.0, pltpu.roll(here, rows - 1, 1))
    pair = bent(here - beyond)
    prior = prior + pair - jnp.where(lane == 0, -bent(here), pltpu.roll(pair, 1, 1))
    beyond = jnp.where(level == depth - 1, 0.0, pltpu.roll(here, depth - 1, 0))
    pair = bent(here - beyond)
    prior = prior + pair - jnp.where(level == 0, -bent(here[:1]), pltpu.roll(pair, 1, 0))
    return here - step_size * prior_weight * prior


def run_of_columns(half_ref, k, first, count, final, store):
    before = half_ref[k, first - 1]
    here = half_ref[k, first]

    def body(i, carry):
        behind, here = carry
        following = half_ref[k, first + i + 1]
        ahead = bent(here - following)
        store(i, settled(here, behind, ahead))
        return ahead, following

    inner = count if final is None else count - 1
    behind, here = lax.fori_loop(0, inner, body, (bent(before - here), here), unroll=2)
    if final is not None:
        store(count - 1, settled(here, behind, bent(here - final)))


def gradient_kernel(groups, pieces, *refs):
    weight_refs = refs[:groups]
    window_refs = refs[groups : 2 * groups]
    volume_ref, half_ref, low_ref, high_ref = refs[2 * groups :]
    _, share, depth, rows = half_ref.shape
    views, cols, _ = weight_refs[0].shape
    chunk = share // pieces
    span = chunk * depth
    windows = [
        jnp.concatenate(
            [jnp.concatenate([ref[v, 0], ref[v, 1]], axis=1) for v in range(views)], axis=0
        )
        for ref in window_refs
    ]
    for i in range(pieces):
        gradient = None
        for g in range(groups):
            product = lax.dot_general(
                weight_refs[g][:, :, i * span : (i + 1) * span].reshape(views * cols, span),
                windows[g],
                (((0,), (0,)), ((), ())),
                preferred_element_type=F32,
            )
            gradient = product if gradient is None else gradient + product
        for k in range(2):
            plane = gradient[:, k * rows : (k + 1) * rows].reshape(chunk, depth, rows)
            held = slice(i * chunk, (i + 1) * chunk)
            half_ref[k, held] = volume_ref[k, held] - step_size * plane
    low_ref[...] = half_ref[:, :1].astype(BF16)
    high_ref[...] = half_ref[:, share - 1 :].astype(BF16)


def half_step_of(weights, windows, volume):
    groups = len(windows)
    _, share, depth, rows = volume.shape
    vmem = pl.BlockSpec(memory_space=VMEM)
    edge = VMEM((2, 1, depth, rows), BF16)
    return pl.pallas_call(
        functools.partial(gradient_kernel, groups, min(4, share)),
        out_shape=(VMEM((2, share, depth, rows), F32), edge, edge),
        in_specs=[vmem] * (2 * groups + 1),
        out_specs=(vmem, vmem, vmem),
        compiler_params=limit(20),
        name="half_step",
    )(*near(*weights, *windows, volume))


def first_kernel(half_ref, part_ref, whole_ref, fresh, sems):
    group = lax.axis_index("view")
    share = half_ref.shape[1]
    puts = []
    for k in range(2):

        def store(i, column):
            fresh[k, i] = column
            part_ref[k, i] = column.astype(BF16)

        run_of_columns(half_ref, k, 1, share // 2, None, store)
        puts.append(
            pltpu.make_async_copy(
                fresh.at[k],
                whole_ref.at[k, pl.ds(group * share + 1, share // 2)],
                sems.at[k],
            )
        )
        puts[-1].start()
    for put in puts:
        put.wait()


def first_part(half, vcols):
    _, share, depth, rows = half.shape
    hbm = pl.BlockSpec(memory_space=pl.ANY)
    vmem = pl.BlockSpec(memory_space=VMEM)
    return pl.pallas_call(
        first_kernel,
        out_shape=(
            VMEM((2, share // 2, depth, rows), BF16),
            jax.ShapeDtypeStruct((2, vcols, depth, rows), F32),
        ),
        in_specs=[vmem],
        out_specs=(vmem, hbm),
        scratch_shapes=[
            VMEM((2, share // 2, depth, rows), F32),
            pltpu.SemaphoreType.DMA((2,)),
        ],
        compiler_params=limit(16),
        name="first_part",
    )(*near(half))


def second_kernel(half_ref, before_ref, after_ref, _, part_ref, whole_ref, fresh, sems):
    group = lax.axis_index("view")
    share = half_ref.shape[1]
    middle = share // 2
    puts = []
    for k in range(2):

        def store(i, column):
            fresh[k, i + 1] = column
            part_ref[k, i + 1] = column.astype(BF16)

        here = half_ref[k, 0]
        column = settled(here, bent(before_ref[k, 0].astype(F32) - here), bent(here - half_ref[k, 1]))
        store(-1, column)
        run_of_columns(half_ref, k, middle + 1, middle - 1, after_ref[k, 0].astype(F32), store)
        for place, (source, target, count) in enumerate(
            ((0, 0, 1), (1, middle + 1, middle - 1))
        ):
            puts.append(
                pltpu.make_async_copy(
                    fresh.at[k, pl.ds(source, count)],
                    whole_ref.at[k, pl.ds(group * share + target, count)],
                    sems.at[k, place],
                )
            )
            puts[-1].start()
    for put in puts:
        put.wait()


def second_part(half, before, after, whole):
    _, share, depth, rows = half.shape
    hbm = pl.BlockSpec(memory_space=pl.ANY)
    vmem = pl.BlockSpec(memory_space=VMEM)
    return pl.pallas_call(
        second_kernel,
        out_shape=(
            VMEM((2, share // 2, depth, rows), BF16),
            jax.ShapeDtypeStruct(whole.shape, F32),
        ),
        in_specs=[vmem, vmem, vmem, hbm],
        out_specs=(vmem, hbm),
        scratch_shapes=[
            VMEM((2, share // 2, depth, rows), F32),
            pltpu.SemaphoreType.DMA((2, 2)),
        ],
        input_output_aliases={3: 1},
        compiler_params=limit(16),
        name="second_part",
    )(*near(half, before, after), whole)


def place_kernel(kinds, groups, *refs):
    parts = refs[: len(kinds)]
    _, whole_ref, fresh, sems = refs[len(kinds) :]
    group = lax.axis_index("view")
    share = whole_ref.shape[1] // groups
    middle = share // 2
    puts = []
    for n, ((second, j), ref) in enumerate(zip(kinds, parts)):
        first = (group ^ j) * share
        runs = ((0, 0, 1), (1, middle + 1, middle - 1)) if second else ((0, 1, middle),)
        for place, (source, target, count) in enumerate(runs):
            for k in range(2):
                fresh[n, k, source : source + count] = ref[k, source : source + count].astype(F32)
                puts.append(
                    pltpu.make_async_copy(
                        fresh.at[n, k, pl.ds(source, count)],
                        whole_ref.at[k, pl.ds(first + target, count)],
                        sems.at[n, k, place],
                    )
                )
                puts[-1].start()
    for put in puts:
        put.wait()


def place(kinds, parts, whole, groups):
    hbm = pl.BlockSpec(memory_space=pl.ANY)
    vmem = pl.BlockSpec(memory_space=VMEM)
    return pl.pallas_call(
        functools.partial(place_kernel, kinds, groups),
        out_shape=jax.ShapeDtypeStruct(whole.shape, F32),
        in_specs=[vmem] * len(parts) + [hbm],
        out_specs=hbm,
        scratch_shapes=[
            VMEM((len(parts),) + parts[0].shape, F32),
            pltpu.SemaphoreType.DMA((len(parts), 2, 2)),
        ],
        input_output_aliases={len(parts): 0},
        compiler_params=limit(16),
        name="place",
    )(*near(*parts), whole)


def per_device(
    object_band,
    dual_band,
    probe_field,
    positions,
    live_counts,
    photon_counts,
    footprints,
    weights,
    volume,
):
    tiles, groups = lax.axis_size("tile"), lax.axis_size("view")
    tile_cols = object_band.shape[2]
    foot_cols = weights.shape[1]
    footprints = footprints[:, 0]
    forward = dft_block(probe_field.shape[1], False)
    inverse = dft_block(probe_field.shape[1], True)

    dealt = deal(weights, groups)
    weight_pieces = [dealt[0]]
    for j in range(1, groups):
        weight_pieces.append(swapped(dealt[j], "view", j))
    keep, send, volume_own = project(footprints, dealt, volume, tiles, tile_cols)
    ahead_one = passed_along(object_band, "tile", -1)
    ahead_two = passed_along(object_band, "tile", -2)
    arrived = swapped(send, "tile", 1)
    projection, *rest = fold(keep, arrived)
    token = rest[-1]
    for n, block in enumerate(rest):
        projection = projection + swapped(block, "tile", 2 * (n + 1)).astype(F32)

    own_update, spill_one, spill_two = patches(
        positions,
        live_counts[:, 0],
        object_band,
        ahead_one,
        ahead_two,
        probe_field,
        forward,
        inverse,
        photon_counts,
        token,
    )
    from_one = passed_along(spill_one, "tile", 1)
    from_two = passed_along(spill_two, "tile", 2)
    summed = own_update + from_one.astype(F32) + from_two.astype(F32)
    object_new = (
        object_band
        + summed[:, 0:2] / (1.0 + summed[:, 2:3])
        - rho_weight * (object_band - projection - dual_band)
    )
    dual_new = dual_band + projection - object_new
    residual = (projection - object_new + dual_band).astype(BF16)

    pieces = [residual]
    for n in range(1, tiles // 2):
        pieces.append(swapped(residual, "tile", 2 * n))
    others = swapped(jnp.stack(pieces), "tile", 1)
    windows = cut(footprints, [piece[None] for piece in pieces] + [others], foot_cols, tiles)
    all_windows = [windows]
    for j in range(1, groups):
        all_windows.append(swapped(windows, "view", j))

    half, low_edge, high_edge = half_step_of(weight_pieces, all_windows, volume_own)
    view_masks = masks_of(groups)
    order = [g * tiles + t for t in range(tiles) for g in range(groups)]
    up = list(zip(order[:-1], order[1:]))
    before = lax.ppermute(high_edge, ("view", "tile"), up)
    after = lax.ppermute(low_edge, ("view", "tile"), [(b, a) for a, b in up])
    part, volume_new = first_part(half, volume.shape[1])
    other, volume_new = second_part(half, before, after, volume_new)
    held = {(False, 0): part, (True, 0): other}
    for masks in zip(view_masks, view_masks[::-1]):
        arrived = {}
        for kind, mask in zip((False, True), masks):
            for (second, j), value in held.items():
                if second == kind:
                    arrived[kind, j ^ mask] = swapped(value, "view", mask)
        held.update(arrived)
    waiting = [key for key in held if key[1]]
    near_keys = [key for key in waiting if key[1] in view_masks]
    rounds = [[key for key in near_keys if not key[0]], [key for key in near_keys if key[0]]]
    far_keys = [key for key in waiting if key not in near_keys]
    rounds += [far_keys[n : n + 2] for n in range(0, len(far_keys), 2)]
    for keys in rounds:
        if keys:
            volume_new = place(keys, [held[key] for key in keys], volume_new, groups)
    return (object_new, dual_new, volume_new)


def solution(mesh):
    return jax.shard_map(
        per_device,
        mesh=mesh,
        in_specs=(
            P("view", None, "tile", None),
            P("view", None, "tile", None),
            P(),
            P("view", "tile"),
            P("view", "tile"),
            P("view", "tile", None, None),
            P("view", "tile"),
            P("view", None, "tile"),
            P(None, "tile", None, None),
        ),
        out_specs=(
            P("view", None, "tile", None),
            P("view", None, "tile", None),
            P(None, "tile", None, None),
        ),
        check_vma=False,
    )
```

```python
import functools
import numpy as np
import jax
import jax.numpy as jnp
from jax import lax
from jax.experimental import pallas as pl
from jax.experimental.pallas import tpu as pltpu
from jax.sharding import PartitionSpec as P


rho_weight = 0.5
step_size = 0.5
prior_weight = 0.5
floor_term = 0.25


F32 = jnp.float32
BF16 = jnp.bfloat16
VMEM = pltpu.VMEM
SMEM = pltpu.SMEM


def passed_along(value, axis, steps):
    count = lax.axis_size(axis)
    initial, last = (max(0, -steps), min(count, count - steps))
    return lax.ppermute(value, axis, [(source, source + steps) for source in range(initial, last)])


def near(*arrays):
    return tuple(pltpu.with_memory_space_constraint(array, VMEM) for array in arrays)


def far(*arrays):
    return tuple(pltpu.with_memory_space_constraint(array, pltpu.HBM) for array in arrays)


def limit(mebibytes):
    return pltpu.CompilerParams(vmem_limit_bytes=mebibytes << 20)


def swapped(value, axis, mask):
    count = lax.axis_size(axis)
    return lax.ppermute(value, axis, [(i, i ^ mask) for i in range(count)])


def masks_of(count):
    return [1 << b for b in range(count.bit_length() - 1)]


def gray(rank):
    return rank ^ (rank >> 1)


def share_at(j, groups):
    rank = lax.axis_index("view") ^ j
    shift = 1
    while shift < groups:
        rank = rank ^ (rank >> shift)
        shift *= 2
    return jnp.where((lax.axis_index("tile") & 1) == 1, groups - 1 - rank, rank)


def dft_block(order_n, inverse):
    counter = np.arange(order_n)
    angles = (counter[:, None] * counter[None, :] % order_n) * (2.0 * np.pi / order_n)
    re = np.cos(angles) / np.sqrt(order_n)
    im = -np.sin(angles) / np.sqrt(order_n)
    im = -im if inverse else im
    return jnp.asarray(np.block([[re, -im], [im, re]]).astype(np.float32)).astype(BF16)


def deal_kernel(groups, offsets, weights_ref, *refs):
    *shares, sems = refs
    copies = []
    for n, (j, ref) in enumerate(zip(offsets, shares)):
        size = ref.shape[2]
        first = pl.multiple_of(share_at(j, groups) * size, size)
        copies.append(
            pltpu.make_async_copy(weights_ref.at[:, :, pl.ds(first, size)], ref, sems.at[n])
        )
        copies[-1].start()
    for copy in copies:
        copy.wait()


def deal(weights, groups, offsets):
    views, cols, voxels = weights.shape
    vmem = pl.BlockSpec(memory_space=VMEM)
    return pl.pallas_call(
        functools.partial(deal_kernel, groups, offsets),
        out_shape=(VMEM((views, cols, voxels // groups), BF16),) * len(offsets),
        in_specs=[pl.BlockSpec(memory_space=pl.ANY)],
        out_specs=(vmem,) * len(offsets),
        scratch_shapes=[pltpu.SemaphoreType.DMA((len(offsets),))],
        compiler_params=limit(8),
        name="deal",
    )(*far(weights))


def ranks(footprints, views, parts, tiles):
    tile = lax.axis_index("tile")
    found = []
    for v in range(views):
        row = []
        for part in range(parts):
            other = (footprints[v] + part) ^ tile
            row.append((other >> 1) + (other & 1) * (tiles // 2))
        found.append(row)
    return found


def project_kernel(pieces, footprints_ref, volume_ref, *refs):
    *shares, keep_ref, send_ref, part_ref, footprints, held, sem, sems = refs
    groups = len(shares)
    views, cols, _ = shares[0].shape
    _, count, depth, rows = part_ref.shape
    half, _, _, width, _ = keep_ref.shape
    chunk = count // pieces
    span = chunk * depth
    spots_copy = pltpu.make_async_copy(footprints_ref, footprints, sem)
    spots_copy.start()
    copies = []
    for j in range(groups):
        first = share_at(j, groups) * count
        for i in range(pieces):
            copies.append(
                pltpu.make_async_copy(
                    volume_ref.at[:, pl.ds(first + i * chunk, chunk)],
                    held.at[j, :, pl.ds(i * chunk, chunk)],
                    sems.at[j, i],
                )
            )
            copies[-1].start()
    keep_ref[...] = jnp.zeros_like(keep_ref)
    send_ref[...] = jnp.zeros_like(send_ref)
    total = jnp.zeros((views * cols, 2 * rows), F32)
    for j, ref in enumerate(shares):
        for i in range(pieces):
            copies[j * pieces + i].wait()
            low = jnp.concatenate(
                [
                    held[j, k, i * chunk : (i + 1) * chunk].reshape(span, rows).astype(BF16)
                    for k in range(2)
                ],
                axis=1,
            )
            total = total + jnp.dot(
                ref[:, :, i * span : (i + 1) * span].reshape(views * cols, span),
                low,
                preferred_element_type=F32,
            )
        if j == 0:
            part_ref[...] = held[0]
    spots_copy.wait()
    spots = ranks(footprints, views, cols // width, 2 * half)
    for v in range(views):
        for part in range(cols // width):
            first = v * cols + part * width
            spot = spots[v][part]
            for ref, wanted, index in (
                (keep_ref, spot < half, spot),
                (send_ref, spot >= half, spot - half),
            ):

                @pl.when(wanted)
                def _():
                    for k in range(2):
                        ref[index, v, k] = total[
                            first : first + width, k * rows : (k + 1) * rows
                        ].astype(BF16)


def project(footprints, shares, volume, tiles, tile_cols):
    groups = len(shares)
    views, _, _ = shares[0].shape
    _, vcols, depth, rows = volume.shape
    count = vcols // groups
    pieces = 2 if count % 2 == 0 else 1
    vmem = pl.BlockSpec(memory_space=VMEM)
    hbm = pl.BlockSpec(memory_space=pl.ANY)
    placed = VMEM((tiles // 2, views, 2, tile_cols, rows), BF16)
    return pl.pallas_call(
        functools.partial(project_kernel, pieces),
        out_shape=(placed, placed, VMEM((2, count, depth, rows), F32)),
        in_specs=[hbm, hbm] + [vmem] * groups,
        out_specs=(vmem,) * 3,
        scratch_shapes=[
            SMEM(footprints.shape, jnp.int32),
            VMEM((groups, 2, count, depth, rows), F32),
            pltpu.SemaphoreType.DMA(()),
            pltpu.SemaphoreType.DMA((groups, pieces)),
        ],
        compiler_params=limit(20),
        name="project",
    )(*far(footprints, volume), *near(*shares))


def fold_kernel(keep_ref, arrived_ref, *refs):
    for n, ref in enumerate(refs):
        ref[...] = (keep_ref[n].astype(F32) + arrived_ref[n].astype(F32)).astype(ref.dtype)


def fold(keep, arrived):
    vmem = pl.BlockSpec(memory_space=VMEM)
    return pl.pallas_call(
        fold_kernel,
        out_shape=tuple(VMEM(keep.shape[1:], BF16 if n else F32) for n in range(keep.shape[0])),
        in_specs=[vmem] * 2,
        out_specs=(vmem,) * keep.shape[0],
        compiler_params=limit(8),
        name="fold",
    )(*near(keep, arrived))


GROUP = 8


def patch_kernel(
    positions,
    live,
    own_ref,
    one_ref,
    two_ref,
    probe_ref,
    forward_ref,
    inverse_ref,
    counts_ref,
    token_ref,
    near_ref,
    ahead_one_ref,
    ahead_two_ref,
    reach,
    total,
    buffer,
    sems,
):
    views, _, width, rows = own_ref.shape
    cols = probe_ref.shape[1]
    span = 3 * width
    for part, ref in enumerate((own_ref, one_ref, two_ref)):
        reach[:, :, part * width : (part + 1) * width, :] = ref[...]
    total[...] = jnp.zeros_like(total)
    starts = [0]
    for v in range(views):
        starts.append(starts[-1] + lax.div(live[v] + (GROUP - 1), GROUP))

    def located(step):
        view, first = 0, 0
        for v in range(1, views):
            after = (step >= starts[v]).astype(jnp.int32)
            view = view + after
            first = jnp.where(after == 1, starts[v], first)
        return view, (step - first) * GROUP

    def fetch(step, slot):
        view, first = located(step)
        return pltpu.make_async_copy(
            counts_ref.at[view, pl.ds(first, GROUP)], buffer.at[slot], sems.at[slot]
        )

    fetch(0, 0).start()

    def body(step, carry):
        slot = step & 1
        view, first = located(step)
        pltpu.make_async_copy(
            counts_ref.at[view, pl.ds(first, GROUP)], buffer.at[slot], sems.at[slot]
        ).wait()

        @pl.when(step + 1 < starts[views])
        def _():
            fetch(step + 1, 1 - slot).start()

        probe_re = probe_ref[0]
        probe_im = probe_ref[1]
        spots = []
        exits = []
        for g in range(GROUP):
            offset = positions[view, first + g]
            spots.append(jnp.where(first + g < live[view], offset, span))
            obj_re = reach[view, 0, pl.ds(offset, cols), :]
            obj_im = reach[view, 1, pl.ds(offset, cols), :]
            wave_re = (probe_re * obj_re - probe_im * obj_im).astype(BF16)
            wave_im = (probe_re * obj_im + probe_im * obj_re).astype(BF16)
            exits.append(jnp.concatenate([wave_re, wave_im], axis=0))
        waves = jnp.concatenate(exits, axis=1)
        done = jnp.dot(forward_ref[...], waves, preferred_element_type=F32).astype(BF16)
        done = jnp.concatenate(
            [
                jnp.concatenate(
                    [
                        done[:cols, g * rows : (g + 1) * rows],
                        done[cols:, g * rows : (g + 1) * rows],
                    ],
                    axis=1,
                )
                for g in range(GROUP)
            ],
            axis=0,
        )
        spectrum = jnp.dot(done, inverse_ref[...], preferred_element_type=F32)
        spec_re = spectrum[:, :rows]
        spec_im = spectrum[:, rows:]
        counts = buffer[slot].reshape(GROUP * cols, rows).astype(F32)
        square = spec_re * spec_re + spec_im * spec_im + floor_term
        factor = (counts * (1.0 / 16.0)) * lax.rsqrt(jnp.maximum(counts * square, 1e-6))
        replaced = jnp.concatenate(
            [(spec_re * factor).astype(BF16), (spec_im * factor).astype(BF16)], axis=1
        )
        back = jnp.dot(replaced, forward_ref[...], preferred_element_type=F32).astype(BF16)
        back = jnp.concatenate(
            [
                jnp.concatenate(
                    [
                        back[g * cols : (g + 1) * cols, :rows],
                        back[g * cols : (g + 1) * cols, rows:],
                    ],
                    axis=0,
                )
                for g in range(GROUP)
            ],
            axis=1,
        )
        wave = jnp.dot(inverse_ref[...], back, preferred_element_type=F32)
        power = probe_re * probe_re + probe_im * probe_im
        for g in range(GROUP):
            diff = wave[:, g * rows : (g + 1) * rows] - exits[g].astype(F32)
            diff_re = diff[:cols]
            diff_im = diff[cols:]
            place = pl.ds(spots[g], cols)
            total[view, 0, place, :] += probe_re * diff_re + probe_im * diff_im
            total[view, 1, place, :] += probe_re * diff_im - probe_im * diff_re
            total[view, 2, place, :] += power
        return carry

    lax.fori_loop(0, starts[views], body, 0)
    near_ref[...] = total[:, :, :width, :]
    for part, ref in ((1, ahead_one_ref), (2, ahead_two_ref)):
        ref[...] = total[:, :, part * width : (part + 1) * width, :].astype(BF16)


def patches(positions, live, own, one, two, probe, forward, inverse, counts, token):
    views, _, width, rows = own.shape
    cols = probe.shape[1]
    slots = counts.shape[1]
    vmem = pl.BlockSpec(memory_space=VMEM)
    smem = pl.BlockSpec(memory_space=SMEM)
    return pl.pallas_call(
        patch_kernel,
        out_shape=(
            VMEM((views, 3, width, rows), F32),
            VMEM((views, 3, width, rows), BF16),
            VMEM((views, 3, width, rows), BF16),
        ),
        in_specs=[smem, smem] + [vmem] * 6 + [pl.BlockSpec(memory_space=pl.ANY)] * 2,
        out_specs=(vmem, vmem, vmem),
        scratch_shapes=[
            VMEM((views, 2, 3 * width, rows), F32),
            VMEM((views, 3, 3 * width + cols, rows), F32),
            VMEM((2, GROUP, cols, rows), jnp.int32),
            pltpu.SemaphoreType.DMA((2,)),
        ],
        compiler_params=limit(20),
        cost_estimate=pl.CostEstimate(
            flops=views * slots * 16 * cols * cols * rows,
            transcendentals=0,
            bytes_accessed=counts.size * 4,
        ),
        name="patches",
    )(positions, live, own, *near(one, two), probe, forward, inverse, counts, *near(token))


def cut_kernel(tiles, footprints, *refs):
    pieces, windows_ref = refs[:-1], refs[-1]
    views, _, cols, _ = windows_ref.shape
    width = pieces[0].shape[3]
    spots = ranks(footprints, views, cols // width, tiles)
    for v in range(views):
        for part in range(cols // width):
            first = 0
            for ref in pieces:
                inside = spots[v][part] - first

                @pl.when((inside >= 0) & (inside < ref.shape[0]))
                def _():
                    windows_ref[v, :, part * width : (part + 1) * width] = ref[inside, v]

                first += ref.shape[0]


def cut(footprints, pieces, cols, tiles):
    _, views, planes, _, rows = pieces[0].shape
    vmem = pl.BlockSpec(memory_space=VMEM)
    return pl.pallas_call(
        functools.partial(cut_kernel, tiles),
        out_shape=VMEM((views, planes, cols, rows), BF16),
        in_specs=[pl.BlockSpec(memory_space=SMEM)] + [vmem] * len(pieces),
        out_specs=vmem,
        compiler_params=limit(8),
        name="cut",
    )(footprints, *near(*pieces))


def bent(d):
    return d * lax.rsqrt(1.0 + d * d)


def settled(here, behind, ahead):
    depth, rows = here.shape
    lane = lax.broadcasted_iota(jnp.int32, (depth, rows), 1)
    level = lax.broadcasted_iota(jnp.int32, (depth, rows), 0)
    prior = ahead - behind
    beyond = jnp.where(lane == rows - 1, 0.0, pltpu.roll(here, rows - 1, 1))
    pair = bent(here - beyond)
    prior = prior + pair - jnp.where(lane == 0, -bent(here), pltpu.roll(pair, 1, 1))
    beyond = jnp.where(level == depth - 1, 0.0, pltpu.roll(here, depth - 1, 0))
    pair = bent(here - beyond)
    prior = prior + pair - jnp.where(level == 0, -bent(here[:1]), pltpu.roll(pair, 1, 0))
    return here - step_size * prior_weight * prior


def run_of_columns(half_ref, k, first, count, store):
    before = half_ref[k, first - 1]
    here = half_ref[k, first]

    def body(i, carry):
        behind, here = carry
        following = half_ref[k, first + i + 1]
        ahead = bent(here - following)
        store(i, settled(here, behind, ahead))
        return ahead, following

    lax.fori_loop(0, count, body, (bent(before - here), here), unroll=2)


def inner_columns(half_ref, part_ref, fresh_ref, first):
    for k in range(2):

        def store(i, column):
            fresh_ref[k, i] = column
            part_ref[k, i] = column.astype(BF16)

        run_of_columns(half_ref, k, first, part_ref.shape[1], store)


def gradient_kernel(groups, pieces, *refs):
    weight_refs = refs[:groups]
    window_refs = refs[groups : 2 * groups]
    volume_ref, half_ref, low_ref, high_ref, part_ref, fresh_ref = refs[2 * groups :]
    _, share, depth, rows = half_ref.shape
    views, cols, _ = weight_refs[0].shape
    chunk = share // pieces
    span = chunk * depth
    windows = [
        jnp.concatenate(
            [jnp.concatenate([ref[v, 0], ref[v, 1]], axis=1) for v in range(views)], axis=0
        )
        for ref in window_refs
    ]
    for i in range(pieces):
        gradient = None
        for g in range(groups):
            product = lax.dot_general(
                weight_refs[g][:, :, i * span : (i + 1) * span].reshape(views * cols, span),
                windows[g],
                (((0,), (0,)), ((), ())),
                preferred_element_type=F32,
            )
            gradient = product if gradient is None else gradient + product
        for k in range(2):
            plane = gradient[:, k * rows : (k + 1) * rows].reshape(chunk, depth, rows)
            held = slice(i * chunk, (i + 1) * chunk)
            half_ref[k, held] = volume_ref[k, held] - step_size * plane
    low_ref[...] = half_ref[:, :1].astype(BF16)
    high_ref[...] = half_ref[:, share - 1 :].astype(BF16)
    inner_columns(half_ref, part_ref, fresh_ref, 1)


def half_step_of(weights, windows, volume):
    groups = len(windows)
    _, share, depth, rows = volume.shape
    vmem = pl.BlockSpec(memory_space=VMEM)
    edge = VMEM((2, 1, depth, rows), BF16)
    inner = (2, share // 2 - 1, depth, rows)
    return pl.pallas_call(
        functools.partial(gradient_kernel, groups, min(4, share)),
        out_shape=(
            VMEM((2, share, depth, rows), F32),
            edge,
            edge,
            VMEM(inner, BF16),
            VMEM(inner, F32),
        ),
        in_specs=[vmem] * (2 * groups + 1),
        out_specs=(vmem,) * 5,
        compiler_params=limit(20),
        name="half_step",
    )(*near(*weights, *windows, volume))


def second_kernel(half_ref, part_ref, fresh_ref):
    inner_columns(half_ref, part_ref, fresh_ref, part_ref.shape[1] + 1)


def second_part(half):
    _, share, depth, rows = half.shape
    vmem = pl.BlockSpec(memory_space=VMEM)
    inner = (2, share // 2 - 1, depth, rows)
    return pl.pallas_call(
        second_kernel,
        out_shape=(VMEM(inner, BF16), VMEM(inner, F32)),
        in_specs=[vmem],
        out_specs=(vmem, vmem),
        compiler_params=limit(16),
        name="second_part",
    )(*near(half))


def third_kernel(half_ref, before_ref, after_ref, first_ref, second_ref, part_ref, whole_ref, *rest):
    edges, sems = rest
    share = half_ref.shape[1]
    inner = first_ref.shape[1]
    start = share_at(0, whole_ref.shape[1] // share) * share
    puts = []

    def put(source, target, count):
        puts.append(
            pltpu.make_async_copy(
                source, whole_ref.at[:, pl.ds(start + target, count)], sems.at[len(puts)]
            )
        )
        puts[-1].start()

    put(first_ref, 1, inner)
    put(second_ref, inner + 1, inner)
    for k in range(2):
        for n, (c, before, after) in enumerate(
            (
                (0, before_ref[k, 0].astype(F32), half_ref[k, 1]),
                (share - 1, half_ref[k, share - 2], after_ref[k, 0].astype(F32)),
            )
        ):
            here = half_ref[k, c]
            column = settled(here, bent(before - here), bent(here - after))
            edges[k, n] = column
            part_ref[k, n] = column.astype(BF16)
    put(edges.at[:, pl.ds(0, 1)], 0, 1)
    put(edges.at[:, pl.ds(1, 1)], share - 1, 1)
    for move in puts:
        move.wait()


def third_part(half, before, after, first, second, vcols):
    _, _, depth, rows = half.shape
    vmem = pl.BlockSpec(memory_space=VMEM)
    return pl.pallas_call(
        third_kernel,
        out_shape=(
            VMEM((2, 2, depth, rows), BF16),
            jax.ShapeDtypeStruct((2, vcols, depth, rows), F32),
        ),
        in_specs=[vmem] * 5,
        out_specs=(vmem, pl.BlockSpec(memory_space=pl.ANY)),
        scratch_shapes=[VMEM((2, 2, depth, rows), F32), pltpu.SemaphoreType.DMA((4,))],
        compiler_params=limit(16),
        name="third_part",
    )(*near(half, before, after, first, second))


def place_kernel(kinds, groups, *refs):
    count = len(kinds)
    parts, whole_ref, fresh, sems = refs[:count], refs[count + 1], refs[count + 2 : -1], refs[-1]
    share = whole_ref.shape[1] // groups
    inner = share // 2 - 1
    puts = []
    for n, ((kind, j), ref) in enumerate(zip(kinds, parts)):
        first = share_at(j, groups) * share
        runs = ((0, 0, 1), (1, share - 1, 1)) if kind == 2 else ((0, kind * inner + 1, inner),)
        for place, (source, target, count) in enumerate(runs):
            for k in range(2):
                fresh[n][k, source : source + count] = ref[k, source : source + count].astype(F32)
                puts.append(
                    pltpu.make_async_copy(
                        fresh[n].at[k, pl.ds(source, count)],
                        whole_ref.at[k, pl.ds(first + target, count)],
                        sems.at[n, k, place],
                    )
                )
                puts[-1].start()
    for put in puts:
        put.wait()


def place(kinds, parts, whole, groups):
    hbm = pl.BlockSpec(memory_space=pl.ANY)
    vmem = pl.BlockSpec(memory_space=VMEM)
    return pl.pallas_call(
        functools.partial(place_kernel, kinds, groups),
        out_shape=jax.ShapeDtypeStruct(whole.shape, F32),
        in_specs=[vmem] * len(parts) + [hbm],
        out_specs=hbm,
        scratch_shapes=[VMEM(part.shape, F32) for part in parts]
        + [pltpu.SemaphoreType.DMA((len(parts), 2, 2))],
        input_output_aliases={len(parts): 0},
        compiler_params=limit(16),
        name="place",
    )(*near(*parts), whole)


def per_device(
    object_band,
    dual_band,
    probe_field,
    positions,
    live_counts,
    photon_counts,
    footprints,
    weights,
    volume,
):
    tiles, groups = lax.axis_size("tile"), lax.axis_size("view")
    tile_cols = object_band.shape[2]
    foot_cols = weights.shape[1]
    footprints = footprints[:, 0]
    forward = dft_block(probe_field.shape[1], False)
    inverse = dft_block(probe_field.shape[1], True)

    view_masks = masks_of(groups)
    later = [j for j in range(groups) if j not in view_masks]
    early_shares = deal(weights, groups, view_masks)
    late_shares = deal(weights, groups, later)
    dealt = dict(zip(view_masks + later, early_shares + late_shares))
    dealt = [dealt[j] for j in range(groups)]
    weight_pieces = [dealt[0]]
    for j in range(1, groups):
        weight_pieces.append(swapped(dealt[j], "view", j))
    keep, send, volume_own = project(footprints, dealt, volume, tiles, tile_cols)
    ahead_one = passed_along(object_band, "tile", -1)
    ahead_two = passed_along(object_band, "tile", -2)
    arrived = swapped(send, "tile", 1)
    projection, *rest = fold(keep, arrived)
    token = rest[-1]
    for n, block in enumerate(rest):
        projection = projection + swapped(block, "tile", 2 * (n + 1)).astype(F32)

    own_update, spill_one, spill_two = patches(
        positions,
        live_counts[:, 0],
        object_band,
        ahead_one,
        ahead_two,
        probe_field,
        forward,
        inverse,
        photon_counts,
        token,
    )
    from_one = passed_along(spill_one, "tile", 1)
    from_two = passed_along(spill_two, "tile", 2)
    summed = own_update + from_one.astype(F32) + from_two.astype(F32)
    object_new = (
        object_band
        + summed[:, 0:2] / (1.0 + summed[:, 2:3])
        - rho_weight * (object_band - projection - dual_band)
    )
    dual_new = dual_band + projection - object_new
    residual = (projection - object_new + dual_band).astype(BF16)

    pieces = [residual]
    for n in range(1, tiles // 2):
        pieces.append(swapped(residual, "tile", 2 * n))
    others = swapped(jnp.stack(pieces), "tile", 1)
    windows = cut(footprints, [piece[None] for piece in pieces] + [others], foot_cols, tiles)
    all_windows = [windows]
    for j in range(1, groups):
        all_windows.append(swapped(windows, "view", j))

    half, low_edge, high_edge, part_a, fresh_a = half_step_of(
        weight_pieces, all_windows, volume_own
    )
    order = []
    for t in range(tiles):
        order += [gray(r) * tiles + t for r in range(groups)][:: -1 if t % 2 else 1]
    up = list(zip(order[:-1], order[1:]))
    before = lax.ppermute(high_edge, ("view", "tile"), up)
    after = lax.ppermute(low_edge, ("view", "tile"), [(b, a) for a, b in up])
    part_b, fresh_b = second_part(half)
    part_c, volume_new = third_part(half, before, after, fresh_a, fresh_b, volume.shape[1])
    held = {(0, 0): part_a, (1, 0): part_b, (2, 0): part_c}
    for masks in zip(view_masks, view_masks[::-1], view_masks):
        arrived = {}
        for (kind, j), value in held.items():
            arrived[kind, j ^ masks[kind]] = swapped(value, "view", masks[kind])
        held.update(arrived)
    rounds = [[(kind, mask) for mask in view_masks] for kind in range(3)]
    far_keys = [j for j in range(1, groups) if j not in view_masks]
    rounds += [[(0, j), (1, j)] for j in far_keys] + [[(2, j)] for j in far_keys]
    for keys in rounds:
        volume_new = place(keys, [held[key] for key in keys], volume_new, groups)
    return (object_new, dual_new, volume_new)


def solution(mesh):
    return jax.shard_map(
        per_device,
        mesh=mesh,
        in_specs=(
            P("view", None, "tile", None),
            P("view", None, "tile", None),
            P(),
            P("view", "tile"),
            P("view", "tile"),
            P("view", "tile", None, None),
            P("view", "tile"),
            P("view", None, "tile"),
            P(None, "tile", None, None),
        ),
        out_specs=(
            P("view", None, "tile", None),
            P("view", None, "tile", None),
            P(None, "tile", None, None),
        ),
        check_vma=False,
    )
```

```python
import functools
import numpy as np
import jax
import jax.numpy as jnp
from jax import lax
from jax.experimental import pallas as pl
from jax.experimental.pallas import tpu as pltpu
from jax.sharding import PartitionSpec as P


rho_weight = 0.5
step_size = 0.5
prior_weight = 0.5
floor_term = 0.25


F32 = jnp.float32
BF16 = jnp.bfloat16
VMEM = pltpu.VMEM
SMEM = pltpu.SMEM


def passed_along(value, axis, steps):
    count = lax.axis_size(axis)
    initial, last = (max(0, -steps), min(count, count - steps))
    return lax.ppermute(value, axis, [(source, source + steps) for source in range(initial, last)])


def near(*arrays):
    return tuple(pltpu.with_memory_space_constraint(array, VMEM) for array in arrays)


def far(*arrays):
    return tuple(pltpu.with_memory_space_constraint(array, pltpu.HBM) for array in arrays)


def limit(mebibytes):
    return pltpu.CompilerParams(vmem_limit_bytes=mebibytes << 20)


def swapped(value, axis, mask):
    count = lax.axis_size(axis)
    return lax.ppermute(value, axis, [(i, i ^ mask) for i in range(count)])


def masks_of(count):
    return [1 << b for b in range(count.bit_length() - 1)]


def gray(rank):
    return rank ^ (rank >> 1)


def share_at(j, groups):
    rank = lax.axis_index("view") ^ j
    shift = 1
    while shift < groups:
        rank = rank ^ (rank >> shift)
        shift *= 2
    return jnp.where((lax.axis_index("tile") & 1) == 1, groups - 1 - rank, rank)


def dft_block(order_n, inverse):
    counter = np.arange(order_n)
    angles = (counter[:, None] * counter[None, :] % order_n) * (2.0 * np.pi / order_n)
    re = np.cos(angles) / np.sqrt(order_n)
    im = -np.sin(angles) / np.sqrt(order_n)
    im = -im if inverse else im
    return jnp.asarray(np.block([[re, -im], [im, re]]).astype(np.float32)).astype(BF16)


def deal_kernel(groups, offsets, weights_ref, *refs):
    *shares, sems = refs
    copies = []
    for n, (j, ref) in enumerate(zip(offsets, shares)):
        size = ref.shape[2]
        first = pl.multiple_of(share_at(j, groups) * size, size)
        copies.append(
            pltpu.make_async_copy(weights_ref.at[:, :, pl.ds(first, size)], ref, sems.at[n])
        )
        copies[-1].start()
    for copy in copies:
        copy.wait()


def deal(weights, groups, offsets):
    views, cols, voxels = weights.shape
    vmem = pl.BlockSpec(memory_space=VMEM)
    return pl.pallas_call(
        functools.partial(deal_kernel, groups, offsets),
        out_shape=(VMEM((views, cols, voxels // groups), BF16),) * len(offsets),
        in_specs=[pl.BlockSpec(memory_space=pl.ANY)],
        out_specs=(vmem,) * len(offsets),
        scratch_shapes=[pltpu.SemaphoreType.DMA((len(offsets),))],
        compiler_params=limit(8),
        name="deal",
    )(*far(weights))


def ranks(footprints, views, parts, tiles):
    tile = lax.axis_index("tile")
    found = []
    for v in range(views):
        row = []
        for part in range(parts):
            other = (footprints[v] + part) ^ tile
            row.append((other >> 1) + (other & 1) * (tiles // 2))
        found.append(row)
    return found


def project_kernel(pieces, footprints_ref, volume_ref, *refs):
    *shares, keep_ref, send_ref, part_ref, footprints, sem = refs
    groups = len(shares)
    views, cols, _ = shares[0].shape
    _, count, depth, rows = part_ref.shape
    half, _, _, width, _ = keep_ref.shape
    chunk = count // pieces
    span = chunk * depth
    spots_copy = pltpu.make_async_copy(footprints_ref, footprints, sem)
    spots_copy.start()
    keep_ref[...] = jnp.zeros_like(keep_ref)
    send_ref[...] = jnp.zeros_like(send_ref)
    total = jnp.zeros((views * cols, 2 * rows), F32)
    for j, ref in enumerate(shares):
        at = share_at(j, groups) * count
        for i in range(pieces):
            low = jnp.concatenate(
                [
                    volume_ref[k, pl.ds(at + i * chunk, chunk)].reshape(span, rows).astype(BF16)
                    for k in range(2)
                ],
                axis=1,
            )
            total = total + jnp.dot(
                ref[:, :, i * span : (i + 1) * span].reshape(views * cols, span),
                low,
                preferred_element_type=F32,
            )
        if j == 0:
            part_ref[...] = volume_ref[:, pl.ds(at, count)]
    spots_copy.wait()
    spots = ranks(footprints, views, cols // width, 2 * half)
    for v in range(views):
        for part in range(cols // width):
            first = v * cols + part * width
            spot = spots[v][part]
            for ref, wanted, index in (
                (keep_ref, spot < half, spot),
                (send_ref, spot >= half, spot - half),
            ):

                @pl.when(wanted)
                def _():
                    for k in range(2):
                        ref[index, v, k] = total[
                            first : first + width, k * rows : (k + 1) * rows
                        ].astype(BF16)


def project(footprints, shares, volume, tiles, tile_cols):
    groups = len(shares)
    views, _, _ = shares[0].shape
    _, vcols, depth, rows = volume.shape
    count = vcols // groups
    pieces = 2 if count % 2 == 0 else 1
    vmem = pl.BlockSpec(memory_space=VMEM)
    hbm = pl.BlockSpec(memory_space=pl.ANY)
    placed = VMEM((tiles // 2, views, 2, tile_cols, rows), BF16)
    return pl.pallas_call(
        functools.partial(project_kernel, pieces),
        out_shape=(placed, placed, VMEM((2, count, depth, rows), F32)),
        in_specs=[hbm, vmem] + [vmem] * groups,
        out_specs=(vmem,) * 3,
        scratch_shapes=[
            SMEM(footprints.shape, jnp.int32),
            pltpu.SemaphoreType.DMA(()),
        ],
        compiler_params=limit(20),
        name="project",
    )(*far(footprints), volume, *near(*shares))


def fold_kernel(keep_ref, arrived_ref, *refs):
    for n, ref in enumerate(refs):
        ref[...] = (keep_ref[n].astype(F32) + arrived_ref[n].astype(F32)).astype(ref.dtype)


def fold(keep, arrived):
    vmem = pl.BlockSpec(memory_space=VMEM)
    return pl.pallas_call(
        fold_kernel,
        out_shape=tuple(VMEM(keep.shape[1:], BF16 if n else F32) for n in range(keep.shape[0])),
        in_specs=[vmem] * 2,
        out_specs=(vmem,) * keep.shape[0],
        compiler_params=limit(8),
        name="fold",
    )(*near(keep, arrived))


GROUP = 8


def patch_kernel(
    positions,
    live,
    own_ref,
    one_ref,
    two_ref,
    probe_ref,
    forward_ref,
    inverse_ref,
    counts_ref,
    token_ref,
    near_ref,
    ahead_one_ref,
    ahead_two_ref,
    reach,
    total,
    buffer,
    sems,
):
    views, _, width, rows = own_ref.shape
    cols = probe_ref.shape[1]
    span = 3 * width
    for part, ref in enumerate((own_ref, one_ref, two_ref)):
        reach[:, :, part * width : (part + 1) * width, :] = ref[...].astype(F32)
    total[...] = jnp.zeros_like(total)
    starts = [0]
    for v in range(views):
        starts.append(starts[-1] + lax.div(live[v] + (GROUP - 1), GROUP))

    def located(step):
        view, first = 0, 0
        for v in range(1, views):
            after = (step >= starts[v]).astype(jnp.int32)
            view = view + after
            first = jnp.where(after == 1, starts[v], first)
        return view, (step - first) * GROUP

    def fetch(step, slot):
        view, first = located(step)
        return pltpu.make_async_copy(
            counts_ref.at[view, pl.ds(first, GROUP)], buffer.at[slot], sems.at[slot]
        )

    fetch(0, 0).start()

    def body(step, carry):
        slot = step & 1
        view, first = located(step)
        pltpu.make_async_copy(
            counts_ref.at[view, pl.ds(first, GROUP)], buffer.at[slot], sems.at[slot]
        ).wait()

        @pl.when(step + 1 < starts[views])
        def _():
            fetch(step + 1, 1 - slot).start()

        probe_re = probe_ref[0]
        probe_im = probe_ref[1]
        spots = []
        exits = []
        for g in range(GROUP):
            offset = positions[view, first + g]
            spots.append(jnp.where(first + g < live[view], offset, span))
            obj_re = reach[view, 0, pl.ds(offset, cols), :]
            obj_im = reach[view, 1, pl.ds(offset, cols), :]
            wave_re = (probe_re * obj_re - probe_im * obj_im).astype(BF16)
            wave_im = (probe_re * obj_im + probe_im * obj_re).astype(BF16)
            exits.append(jnp.concatenate([wave_re, wave_im], axis=0))
        waves = jnp.concatenate(exits, axis=1)
        done = jnp.dot(forward_ref[...], waves, preferred_element_type=F32).astype(BF16)
        done = jnp.concatenate(
            [
                jnp.concatenate(
                    [
                        done[:cols, g * rows : (g + 1) * rows],
                        done[cols:, g * rows : (g + 1) * rows],
                    ],
                    axis=1,
                )
                for g in range(GROUP)
            ],
            axis=0,
        )
        spectrum = jnp.dot(done, inverse_ref[...], preferred_element_type=F32)
        spec_re = spectrum[:, :rows]
        spec_im = spectrum[:, rows:]
        counts = buffer[slot].reshape(GROUP * cols, rows).astype(F32)
        square = spec_re * spec_re + spec_im * spec_im + floor_term
        factor = (counts * (1.0 / 16.0)) * lax.rsqrt(jnp.maximum(counts * square, 1e-6))
        replaced = jnp.concatenate(
            [(spec_re * factor).astype(BF16), (spec_im * factor).astype(BF16)], axis=1
        )
        back = jnp.dot(replaced, forward_ref[...], preferred_element_type=F32).astype(BF16)
        back = jnp.concatenate(
            [
                jnp.concatenate(
                    [
                        back[g * cols : (g + 1) * cols, :rows],
                        back[g * cols : (g + 1) * cols, rows:],
                    ],
                    axis=0,
                )
                for g in range(GROUP)
            ],
            axis=1,
        )
        wave = jnp.dot(inverse_ref[...], back, preferred_element_type=F32)
        power = probe_re * probe_re + probe_im * probe_im
        for g in range(GROUP):
            diff = wave[:, g * rows : (g + 1) * rows] - exits[g].astype(F32)
            diff_re = diff[:cols]
            diff_im = diff[cols:]
            place = pl.ds(spots[g], cols)
            total[view, 0, place, :] += probe_re * diff_re + probe_im * diff_im
            total[view, 1, place, :] += probe_re * diff_im - probe_im * diff_re
            total[view, 2, place, :] += power
        return carry

    lax.fori_loop(0, starts[views], body, 0)
    near_ref[...] = total[:, :, :width, :]
    for part, ref in ((1, ahead_one_ref), (2, ahead_two_ref)):
        ref[...] = total[:, :, part * width : (part + 1) * width, :].astype(BF16)


def patches(positions, live, own, one, two, probe, forward, inverse, counts, token):
    views, _, width, rows = own.shape
    cols = probe.shape[1]
    slots = counts.shape[1]
    vmem = pl.BlockSpec(memory_space=VMEM)
    smem = pl.BlockSpec(memory_space=SMEM)
    return pl.pallas_call(
        patch_kernel,
        out_shape=(
            VMEM((views, 3, width, rows), F32),
            VMEM((views, 3, width, rows), BF16),
            VMEM((views, 3, width, rows), BF16),
        ),
        in_specs=[smem, smem] + [vmem] * 6 + [pl.BlockSpec(memory_space=pl.ANY)] * 2,
        out_specs=(vmem, vmem, vmem),
        scratch_shapes=[
            VMEM((views, 2, 3 * width, rows), F32),
            VMEM((views, 3, 3 * width + cols, rows), F32),
            VMEM((2, GROUP, cols, rows), jnp.int32),
            pltpu.SemaphoreType.DMA((2,)),
        ],
        compiler_params=limit(20),
        cost_estimate=pl.CostEstimate(
            flops=views * slots * 16 * cols * cols * rows,
            transcendentals=0,
            bytes_accessed=counts.size * 4,
        ),
        name="patches",
    )(positions, live, own, *near(one, two), probe, forward, inverse, counts, *near(token))


def cut_kernel(tiles, footprints, *refs):
    pieces, windows_ref = refs[:-1], refs[-1]
    views, _, cols, _ = windows_ref.shape
    width = pieces[0].shape[3]
    spots = ranks(footprints, views, cols // width, tiles)
    for v in range(views):
        for part in range(cols // width):
            first = 0
            for ref in pieces:
                inside = spots[v][part] - first

                @pl.when((inside >= 0) & (inside < ref.shape[0]))
                def _():
                    windows_ref[v, :, part * width : (part + 1) * width] = ref[inside, v]

                first += ref.shape[0]


def cut(footprints, pieces, cols, tiles):
    _, views, planes, _, rows = pieces[0].shape
    vmem = pl.BlockSpec(memory_space=VMEM)
    return pl.pallas_call(
        functools.partial(cut_kernel, tiles),
        out_shape=VMEM((views, planes, cols, rows), BF16),
        in_specs=[pl.BlockSpec(memory_space=SMEM)] + [vmem] * len(pieces),
        out_specs=vmem,
        compiler_params=limit(8),
        name="cut",
    )(footprints, *near(*pieces))


def inner_runs(share):
    first = max(1, share // 2 - 2)
    return ((1, first), (1 + first, share - 2 - first))


def bent(d):
    return d * lax.rsqrt(1.0 + d * d)


def settled(here, behind, ahead):
    depth, rows = here.shape
    lane = lax.broadcasted_iota(jnp.int32, (depth, rows), 1)
    level = lax.broadcasted_iota(jnp.int32, (depth, rows), 0)
    prior = ahead - behind
    beyond = jnp.where(lane == rows - 1, 0.0, pltpu.roll(here, rows - 1, 1))
    pair = bent(here - beyond)
    prior = prior + pair - jnp.where(lane == 0, -bent(here), pltpu.roll(pair, 1, 1))
    beyond = jnp.where(level == depth - 1, 0.0, pltpu.roll(here, depth - 1, 0))
    pair = bent(here - beyond)
    prior = prior + pair - jnp.where(level == 0, -bent(here[:1]), pltpu.roll(pair, 1, 0))
    return here - step_size * prior_weight * prior


def run_of_columns(half_ref, k, first, count, store):
    before = half_ref[k, first - 1]
    here = half_ref[k, first]

    def body(i, carry):
        behind, here = carry
        following = half_ref[k, first + i + 1]
        ahead = bent(here - following)
        store(i, settled(here, behind, ahead))
        return ahead, following

    lax.fori_loop(0, count, body, (bent(before - here), here), unroll=2)


def inner_columns(half_ref, part_ref, fresh_ref, first):
    for k in range(2):

        def store(i, column):
            fresh_ref[k, i] = column
            part_ref[k, i] = column.astype(BF16)

        run_of_columns(half_ref, k, first, part_ref.shape[1], store)


def gradient_kernel(groups, pieces, *refs):
    weight_refs = refs[:groups]
    window_refs = refs[groups : 2 * groups]
    volume_ref, half_ref, low_ref, high_ref, part_ref, fresh_ref = refs[2 * groups :]
    _, share, depth, rows = half_ref.shape
    views, cols, _ = weight_refs[0].shape
    chunk = share // pieces
    span = chunk * depth
    windows = [
        jnp.concatenate(
            [jnp.concatenate([ref[v, 0], ref[v, 1]], axis=1) for v in range(views)], axis=0
        )
        for ref in window_refs
    ]
    for i in range(pieces):
        gradient = None
        for g in range(groups):
            product = lax.dot_general(
                weight_refs[g][:, :, i * span : (i + 1) * span].reshape(views * cols, span),
                windows[g],
                (((0,), (0,)), ((), ())),
                preferred_element_type=F32,
            )
            gradient = product if gradient is None else gradient + product
        for k in range(2):
            plane = gradient[:, k * rows : (k + 1) * rows].reshape(chunk, depth, rows)
            held = slice(i * chunk, (i + 1) * chunk)
            half_ref[k, held] = volume_ref[k, held] - step_size * plane
    low_ref[...] = half_ref[:, :1].astype(BF16)
    high_ref[...] = half_ref[:, share - 1 :].astype(BF16)
    inner_columns(half_ref, part_ref, fresh_ref, inner_runs(share)[0][0])


def half_step_of(weights, windows, volume):
    groups = len(windows)
    _, share, depth, rows = volume.shape
    vmem = pl.BlockSpec(memory_space=VMEM)
    edge = VMEM((2, 1, depth, rows), BF16)
    inner = (2, inner_runs(share)[0][1], depth, rows)
    return pl.pallas_call(
        functools.partial(gradient_kernel, groups, min(4, share)),
        out_shape=(
            VMEM((2, share, depth, rows), F32),
            edge,
            edge,
            VMEM(inner, BF16),
            VMEM(inner, F32),
        ),
        in_specs=[vmem] * (2 * groups + 1),
        out_specs=(vmem,) * 5,
        compiler_params=limit(20),
        name="half_step",
    )(*near(*weights, *windows, volume))


def second_kernel(half_ref, part_ref, fresh_ref):
    inner_columns(half_ref, part_ref, fresh_ref, inner_runs(half_ref.shape[1])[1][0])


def second_part(half):
    _, share, depth, rows = half.shape
    vmem = pl.BlockSpec(memory_space=VMEM)
    inner = (2, inner_runs(share)[1][1], depth, rows)
    return pl.pallas_call(
        second_kernel,
        out_shape=(VMEM(inner, BF16), VMEM(inner, F32)),
        in_specs=[vmem],
        out_specs=(vmem, vmem),
        compiler_params=limit(16),
        name="second_part",
    )(*near(half))


def third_kernel(half_ref, before_ref, after_ref, first_ref, second_ref, part_ref, whole_ref, *rest):
    edges, sems = rest
    share = half_ref.shape[1]
    start = share_at(0, whole_ref.shape[1] // share) * share
    puts = []

    def put(source, target, count):
        puts.append(
            pltpu.make_async_copy(
                source, whole_ref.at[:, pl.ds(start + target, count)], sems.at[len(puts)]
            )
        )
        puts[-1].start()

    for ref, run in zip((first_ref, second_ref), inner_runs(share)):
        put(ref, *run)
    for k in range(2):
        for n, (c, before, after) in enumerate(
            (
                (0, before_ref[k, 0].astype(F32), half_ref[k, 1]),
                (share - 1, half_ref[k, share - 2], after_ref[k, 0].astype(F32)),
            )
        ):
            here = half_ref[k, c]
            column = settled(here, bent(before - here), bent(here - after))
            edges[k, n] = column
            part_ref[k, n] = column.astype(BF16)
    put(edges.at[:, pl.ds(0, 1)], 0, 1)
    put(edges.at[:, pl.ds(1, 1)], share - 1, 1)
    for move in puts:
        move.wait()


def third_part(half, before, after, first, second, vcols):
    _, _, depth, rows = half.shape
    vmem = pl.BlockSpec(memory_space=VMEM)
    return pl.pallas_call(
        third_kernel,
        out_shape=(
            VMEM((2, 2, depth, rows), BF16),
            jax.ShapeDtypeStruct((2, vcols, depth, rows), F32),
        ),
        in_specs=[vmem] * 5,
        out_specs=(vmem, pl.BlockSpec(memory_space=pl.ANY)),
        scratch_shapes=[VMEM((2, 2, depth, rows), F32), pltpu.SemaphoreType.DMA((4,))],
        compiler_params=limit(16),
        name="third_part",
    )(*near(half, before, after, first, second))


def place_kernel(kinds, groups, *refs):
    count = len(kinds)
    parts, whole_ref, fresh, sems = refs[:count], refs[count + 1], refs[count + 2 : -1], refs[-1]
    share = whole_ref.shape[1] // groups
    puts = []
    for n, ((kind, j), ref) in enumerate(zip(kinds, parts)):
        first = share_at(j, groups) * share
        runs = ((0, 0, 1), (1, share - 1, 1)) if kind == 2 else ((0, *inner_runs(share)[kind]),)
        for place, (source, target, count) in enumerate(runs):
            for k in range(2):
                fresh[n][k, source : source + count] = ref[k, source : source + count].astype(F32)
                puts.append(
                    pltpu.make_async_copy(
                        fresh[n].at[k, pl.ds(source, count)],
                        whole_ref.at[k, pl.ds(first + target, count)],
                        sems.at[n, k, place],
                    )
                )
                puts[-1].start()
    for put in puts:
        put.wait()


def place(kinds, parts, whole, groups):
    hbm = pl.BlockSpec(memory_space=pl.ANY)
    vmem = pl.BlockSpec(memory_space=VMEM)
    return pl.pallas_call(
        functools.partial(place_kernel, kinds, groups),
        out_shape=jax.ShapeDtypeStruct(whole.shape, F32),
        in_specs=[vmem] * len(parts) + [hbm],
        out_specs=hbm,
        scratch_shapes=[VMEM(part.shape, F32) for part in parts]
        + [pltpu.SemaphoreType.DMA((len(parts), 2, 2))],
        input_output_aliases={len(parts): 0},
        compiler_params=limit(16),
        name="place",
    )(*near(*parts), whole)


def per_device(
    object_band,
    dual_band,
    probe_field,
    positions,
    live_counts,
    photon_counts,
    footprints,
    weights,
    volume,
):
    tiles, groups = lax.axis_size("tile"), lax.axis_size("view")
    tile_cols = object_band.shape[2]
    foot_cols = weights.shape[1]
    footprints = footprints[:, 0]
    forward = dft_block(probe_field.shape[1], False)
    inverse = dft_block(probe_field.shape[1], True)

    view_masks = masks_of(groups)
    later = [j for j in range(groups) if j not in view_masks]
    object_low = object_band.astype(BF16)
    early_shares = deal(weights, groups, view_masks)
    late_shares = deal(weights, groups, later)
    dealt = dict(zip(view_masks + later, early_shares + late_shares))
    dealt = [dealt[j] for j in range(groups)]
    weight_pieces = [dealt[0]]
    for j in range(1, groups):
        weight_pieces.append(swapped(dealt[j], "view", j))
    keep, send, volume_own = project(footprints, dealt, volume, tiles, tile_cols)
    ahead_one = passed_along(object_low, "tile", -1)
    ahead_two = passed_along(object_low, "tile", -2)
    arrived = swapped(send, "tile", 1)
    projection, *rest = fold(keep, arrived)
    token = rest[-1]
    for n, block in enumerate(rest):
        projection = projection + swapped(block, "tile", 2 * (n + 1)).astype(F32)

    own_update, spill_one, spill_two = patches(
        positions,
        live_counts[:, 0],
        object_band,
        ahead_one,
        ahead_two,
        probe_field,
        forward,
        inverse,
        photon_counts,
        token,
    )
    from_one = passed_along(spill_one, "tile", 1)
    from_two = passed_along(spill_two, "tile", 2)
    summed = own_update + from_one.astype(F32) + from_two.astype(F32)
    object_new = (
        object_band
        + summed[:, 0:2] / (1.0 + summed[:, 2:3])
        - rho_weight * (object_band - projection - dual_band)
    )
    dual_new = dual_band + projection - object_new
    residual = (projection - object_new + dual_band).astype(BF16)

    pieces = [residual]
    for n in range(1, tiles // 2):
        pieces.append(swapped(residual, "tile", 2 * n))
    others = swapped(jnp.stack(pieces), "tile", 1)
    windows = cut(footprints, [piece[None] for piece in pieces] + [others], foot_cols, tiles)
    all_windows = [windows]
    for j in range(1, groups):
        all_windows.append(swapped(windows, "view", j))

    half, low_edge, high_edge, part_a, fresh_a = half_step_of(
        weight_pieces, all_windows, volume_own
    )
    order = []
    for t in range(tiles):
        order += [gray(r) * tiles + t for r in range(groups)][:: -1 if t % 2 else 1]
    up = list(zip(order[:-1], order[1:]))
    before = lax.ppermute(high_edge, ("view", "tile"), up)
    after = lax.ppermute(low_edge, ("view", "tile"), [(b, a) for a, b in up])
    part_b, fresh_b = second_part(half)
    part_c, volume_new = third_part(half, before, after, fresh_a, fresh_b, volume.shape[1])
    held = {(0, 0): part_a, (1, 0): part_b, (2, 0): part_c}
    for masks in zip(view_masks, view_masks[::-1], view_masks):
        arrived = {}
        for (kind, j), value in held.items():
            arrived[kind, j ^ masks[kind]] = swapped(value, "view", masks[kind])
        held.update(arrived)
    rounds = [[(kind, mask) for mask in view_masks] for kind in range(3)]
    far_keys = [j for j in range(1, groups) if j not in view_masks]
    rounds += [[(0, j)] for j in far_keys] + [[(2, j), (1, j)] for j in far_keys]
    for keys in rounds:
        volume_new = place(keys, [held[key] for key in keys], volume_new, groups)
    return (object_new, dual_new, volume_new)


def solution(mesh):
    return jax.shard_map(
        per_device,
        mesh=mesh,
        in_specs=(
            P("view", None, "tile", None),
            P("view", None, "tile", None),
            P(),
            P("view", "tile"),
            P("view", "tile"),
            P("view", "tile", None, None),
            P("view", "tile"),
            P("view", None, "tile"),
            P(None, "tile", None, None),
        ),
        out_specs=(
            P("view", None, "tile", None),
            P("view", None, "tile", None),
            P(None, "tile", None, None),
        ),
        check_vma=False,
    )
```

```python
import functools
import numpy as np
import jax
import jax.numpy as jnp
from jax import lax
from jax.experimental import pallas as pl
from jax.experimental.pallas import tpu as pltpu
from jax.sharding import PartitionSpec as P


rho_weight = 0.5
step_size = 0.5
prior_weight = 0.5
floor_term = 0.25


F32 = jnp.float32
BF16 = jnp.bfloat16
VMEM = pltpu.VMEM
SMEM = pltpu.SMEM


def passed_along(value, axis, steps):
    count = lax.axis_size(axis)
    initial, last = (max(0, -steps), min(count, count - steps))
    return lax.ppermute(value, axis, [(source, source + steps) for source in range(initial, last)])


def near(*arrays):
    return tuple(pltpu.with_memory_space_constraint(array, VMEM) for array in arrays)


def far(*arrays):
    return tuple(pltpu.with_memory_space_constraint(array, pltpu.HBM) for array in arrays)


def limit(mebibytes):
    return pltpu.CompilerParams(vmem_limit_bytes=mebibytes << 20)


def window_order(groups):
    masks = masks_of(groups)
    return masks[-1:] + [j for j in range(1, groups) if j not in masks] + masks[:-1]


def swapped(value, axis, mask):
    count = lax.axis_size(axis)
    return lax.ppermute(value, axis, [(i, i ^ mask) for i in range(count)])


def masks_of(count):
    return [1 << b for b in range(count.bit_length() - 1)]


def gray(rank):
    return rank ^ (rank >> 1)


def share_at(j, groups):
    rank = lax.axis_index("view") ^ j
    shift = 1
    while shift < groups:
        rank = rank ^ (rank >> shift)
        shift *= 2
    return jnp.where((lax.axis_index("tile") & 1) == 1, groups - 1 - rank, rank)


def dft_block(order_n, inverse):
    counter = np.arange(order_n)
    angles = (counter[:, None] * counter[None, :] % order_n) * (2.0 * np.pi / order_n)
    re = np.cos(angles) / np.sqrt(order_n)
    im = -np.sin(angles) / np.sqrt(order_n)
    im = -im if inverse else im
    return jnp.asarray(np.block([[re, -im], [im, re]]).astype(np.float32)).astype(BF16)


def deal_kernel(groups, offsets, weights_ref, *refs):
    *shares, sems = refs
    copies = []
    for n, (j, ref) in enumerate(zip(offsets, shares)):
        size = ref.shape[2]
        first = pl.multiple_of(share_at(j, groups) * size, size)
        copies.append(
            pltpu.make_async_copy(weights_ref.at[:, :, pl.ds(first, size)], ref, sems.at[n])
        )
        copies[-1].start()
    for copy in copies:
        copy.wait()


def deal(weights, groups, offsets):
    views, cols, voxels = weights.shape
    vmem = pl.BlockSpec(memory_space=VMEM)
    return pl.pallas_call(
        functools.partial(deal_kernel, groups, offsets),
        out_shape=(VMEM((views, cols, voxels // groups), BF16),) * len(offsets),
        in_specs=[pl.BlockSpec(memory_space=pl.ANY)],
        out_specs=(vmem,) * len(offsets),
        scratch_shapes=[pltpu.SemaphoreType.DMA((len(offsets),))],
        compiler_params=limit(8),
        name="deal",
    )(*far(weights))


def ranks(footprints, views, parts, tiles):
    tile = lax.axis_index("tile")
    found = []
    for v in range(views):
        row = []
        for part in range(parts):
            other = (footprints[v] + part) ^ tile
            row.append((other >> 1) + (other & 1) * (tiles // 2))
        found.append(row)
    return found


def project_kernel(pieces, footprints_ref, volume_ref, *refs):
    *shares, keep_ref, send_ref, part_ref, footprints, sem = refs
    groups = len(shares)
    views, cols, _ = shares[0].shape
    _, count, depth, rows = part_ref.shape
    half, _, _, width, _ = keep_ref.shape
    chunk = count // pieces
    span = chunk * depth
    spots_copy = pltpu.make_async_copy(footprints_ref, footprints, sem)
    spots_copy.start()
    keep_ref[...] = jnp.zeros_like(keep_ref)
    send_ref[...] = jnp.zeros_like(send_ref)
    total = jnp.zeros((views * cols, 2 * rows), F32)
    for j, ref in enumerate(shares):
        at = share_at(j, groups) * count
        for i in range(pieces):
            low = jnp.concatenate(
                [
                    volume_ref[k, pl.ds(at + i * chunk, chunk)].reshape(span, rows).astype(BF16)
                    for k in range(2)
                ],
                axis=1,
            )
            total = total + jnp.dot(
                ref[:, :, i * span : (i + 1) * span].reshape(views * cols, span),
                low,
                preferred_element_type=F32,
            )
        if j == 0:
            part_ref[...] = volume_ref[:, pl.ds(at, count)]
    spots_copy.wait()
    spots = ranks(footprints, views, cols // width, 2 * half)
    for v in range(views):
        for part in range(cols // width):
            first = v * cols + part * width
            spot = spots[v][part]
            for ref, wanted, index in (
                (keep_ref, spot < half, spot),
                (send_ref, spot >= half, spot - half),
            ):

                @pl.when(wanted)
                def _():
                    for k in range(2):
                        ref[index, v, k] = total[
                            first : first + width, k * rows : (k + 1) * rows
                        ].astype(BF16)


def project(footprints, shares, volume, tiles, tile_cols):
    groups = len(shares)
    views, _, _ = shares[0].shape
    _, vcols, depth, rows = volume.shape
    count = vcols // groups
    pieces = 2 if count % 2 == 0 else 1
    vmem = pl.BlockSpec(memory_space=VMEM)
    hbm = pl.BlockSpec(memory_space=pl.ANY)
    placed = VMEM((tiles // 2, views, 2, tile_cols, rows), BF16)
    return pl.pallas_call(
        functools.partial(project_kernel, pieces),
        out_shape=(placed, placed, VMEM((2, count, depth, rows), F32)),
        in_specs=[hbm, vmem] + [vmem] * groups,
        out_specs=(vmem,) * 3,
        scratch_shapes=[
            SMEM(footprints.shape, jnp.int32),
            pltpu.SemaphoreType.DMA(()),
        ],
        compiler_params=limit(20),
        name="project",
    )(*far(footprints), volume, *near(*shares))


def fold_kernel(keep_ref, arrived_ref, near_ref, send_ref):
    half = near_ref.shape[0]
    near_ref[...] = keep_ref[:half].astype(F32) + arrived_ref[:half].astype(F32)
    send_ref[...] = (keep_ref[half:].astype(F32) + arrived_ref[half:].astype(F32)).astype(BF16)


def fold(keep, arrived):
    vmem = pl.BlockSpec(memory_space=VMEM)
    shape = (keep.shape[0] // 2,) + keep.shape[1:]
    return pl.pallas_call(
        fold_kernel,
        out_shape=(VMEM(shape, F32), VMEM(shape, BF16)),
        in_specs=[vmem] * 2,
        out_specs=(vmem,) * 2,
        compiler_params=limit(8),
        name="fold",
    )(*near(keep, arrived))


GROUP = 8


def patch_kernel(
    positions,
    live,
    own_ref,
    one_ref,
    two_ref,
    probe_ref,
    forward_ref,
    inverse_ref,
    counts_ref,
    token_ref,
    near_ref,
    ahead_one_ref,
    ahead_two_ref,
    reach,
    total,
    buffer,
    sems,
):
    views, _, width, rows = own_ref.shape
    cols = probe_ref.shape[1]
    span = 3 * width
    for part, ref in enumerate((own_ref, one_ref, two_ref)):
        reach[:, :, part * width : (part + 1) * width, :] = ref[...].astype(F32)
    total[...] = jnp.zeros_like(total)
    starts = [0]
    for v in range(views):
        starts.append(starts[-1] + lax.div(live[v] + (GROUP - 1), GROUP))

    def located(step):
        view, first = 0, 0
        for v in range(1, views):
            after = (step >= starts[v]).astype(jnp.int32)
            view = view + after
            first = jnp.where(after == 1, starts[v], first)
        return view, (step - first) * GROUP

    def fetch(step, slot):
        view, first = located(step)
        return pltpu.make_async_copy(
            counts_ref.at[view, pl.ds(first, GROUP)], buffer.at[slot], sems.at[slot]
        )

    fetch(0, 0).start()

    def body(step, carry):
        slot = step & 1
        view, first = located(step)
        pltpu.make_async_copy(
            counts_ref.at[view, pl.ds(first, GROUP)], buffer.at[slot], sems.at[slot]
        ).wait()

        @pl.when(step + 1 < starts[views])
        def _():
            fetch(step + 1, 1 - slot).start()

        probe_re = probe_ref[0]
        probe_im = probe_ref[1]
        spots = []
        exits = []
        for g in range(GROUP):
            offset = positions[view, first + g]
            spots.append(jnp.where(first + g < live[view], offset, span))
            obj_re = reach[view, 0, pl.ds(offset, cols), :]
            obj_im = reach[view, 1, pl.ds(offset, cols), :]
            wave_re = (probe_re * obj_re - probe_im * obj_im).astype(BF16)
            wave_im = (probe_re * obj_im + probe_im * obj_re).astype(BF16)
            exits.append(jnp.concatenate([wave_re, wave_im], axis=0))
        waves = jnp.concatenate(exits, axis=1)
        done = jnp.dot(forward_ref[...], waves, preferred_element_type=F32).astype(BF16)
        done = jnp.concatenate(
            [
                jnp.concatenate(
                    [
                        done[:cols, g * rows : (g + 1) * rows],
                        done[cols:, g * rows : (g + 1) * rows],
                    ],
                    axis=1,
                )
                for g in range(GROUP)
            ],
            axis=0,
        )
        spectrum = jnp.dot(done, inverse_ref[...], preferred_element_type=F32)
        spec_re = spectrum[:, :rows]
        spec_im = spectrum[:, rows:]
        counts = buffer[slot].reshape(GROUP * cols, rows).astype(F32)
        square = spec_re * spec_re + spec_im * spec_im + floor_term
        factor = (counts * (1.0 / 16.0)) * lax.rsqrt(jnp.maximum(counts * square, 1e-6))
        replaced = jnp.concatenate(
            [(spec_re * factor).astype(BF16), (spec_im * factor).astype(BF16)], axis=1
        )
        back = jnp.dot(replaced, forward_ref[...], preferred_element_type=F32).astype(BF16)
        back = jnp.concatenate(
            [
                jnp.concatenate(
                    [
                        back[g * cols : (g + 1) * cols, :rows],
                        back[g * cols : (g + 1) * cols, rows:],
                    ],
                    axis=0,
                )
                for g in range(GROUP)
            ],
            axis=1,
        )
        wave = jnp.dot(inverse_ref[...], back, preferred_element_type=F32)
        power = probe_re * probe_re + probe_im * probe_im
        for g in range(GROUP):
            diff = wave[:, g * rows : (g + 1) * rows] - exits[g].astype(F32)
            diff_re = diff[:cols]
            diff_im = diff[cols:]
            place = pl.ds(spots[g], cols)
            total[view, 0, place, :] += probe_re * diff_re + probe_im * diff_im
            total[view, 1, place, :] += probe_re * diff_im - probe_im * diff_re
            total[view, 2, place, :] += power
        return carry

    lax.fori_loop(0, starts[views], body, 0)
    near_ref[...] = total[:, :, :width, :]
    for part, ref in ((1, ahead_one_ref), (2, ahead_two_ref)):
        ref[...] = total[:, :, part * width : (part + 1) * width, :].astype(BF16)


def patches(positions, live, own, one, two, probe, forward, inverse, counts, token):
    views, _, width, rows = own.shape
    cols = probe.shape[1]
    slots = counts.shape[1]
    vmem = pl.BlockSpec(memory_space=VMEM)
    smem = pl.BlockSpec(memory_space=SMEM)
    return pl.pallas_call(
        patch_kernel,
        out_shape=(
            VMEM((views, 3, width, rows), F32),
            VMEM((views, 3, width, rows), BF16),
            VMEM((views, 3, width, rows), BF16),
        ),
        in_specs=[smem, smem] + [vmem] * 6 + [pl.BlockSpec(memory_space=pl.ANY)] * 2,
        out_specs=(vmem, vmem, vmem),
        scratch_shapes=[
            VMEM((views, 2, 3 * width, rows), F32),
            VMEM((views, 3, 3 * width + cols, rows), F32),
            VMEM((2, GROUP, cols, rows), jnp.int32),
            pltpu.SemaphoreType.DMA((2,)),
        ],
        compiler_params=limit(20),
        cost_estimate=pl.CostEstimate(
            flops=views * slots * 16 * cols * cols * rows,
            transcendentals=0,
            bytes_accessed=counts.size * 4,
        ),
        name="patches",
    )(positions, live, own, *near(one, two), probe, forward, inverse, counts, *near(token))


def cut_kernel(tiles, footprints, *refs):
    pieces, windows_ref = refs[:-1], refs[-1]
    views, _, cols, _ = windows_ref.shape
    width = pieces[0].shape[3]
    spots = ranks(footprints, views, cols // width, tiles)
    for v in range(views):
        for part in range(cols // width):
            first = 0
            for ref in pieces:
                inside = spots[v][part] - first

                @pl.when((inside >= 0) & (inside < ref.shape[0]))
                def _():
                    windows_ref[v, :, part * width : (part + 1) * width] = ref[inside, v]

                first += ref.shape[0]


def cut(footprints, pieces, cols, tiles):
    _, views, planes, _, rows = pieces[0].shape
    vmem = pl.BlockSpec(memory_space=VMEM)
    return pl.pallas_call(
        functools.partial(cut_kernel, tiles),
        out_shape=VMEM((views, planes, cols, rows), BF16),
        in_specs=[pl.BlockSpec(memory_space=SMEM)] + [vmem] * len(pieces),
        out_specs=vmem,
        compiler_params=limit(8),
        name="cut",
    )(footprints, *near(*pieces))


def inner_runs(share):
    first = max(1, share // 2 - 2)
    return ((1, first), (1 + first, share - 2 - first))


def bent(d):
    return d * lax.rsqrt(1.0 + d * d)


def settled(here, behind, ahead):
    depth, rows = here.shape
    lane = lax.broadcasted_iota(jnp.int32, (depth, rows), 1)
    level = lax.broadcasted_iota(jnp.int32, (depth, rows), 0)
    prior = ahead - behind
    beyond = jnp.where(lane == rows - 1, 0.0, pltpu.roll(here, rows - 1, 1))
    pair = bent(here - beyond)
    prior = prior + pair - jnp.where(lane == 0, -bent(here), pltpu.roll(pair, 1, 1))
    beyond = jnp.where(level == depth - 1, 0.0, pltpu.roll(here, depth - 1, 0))
    pair = bent(here - beyond)
    prior = prior + pair - jnp.where(level == 0, -bent(here[:1]), pltpu.roll(pair, 1, 0))
    return here - step_size * prior_weight * prior


def run_of_columns(half_ref, k, first, count, store):
    before = half_ref[k, first - 1]
    here = half_ref[k, first]

    def body(i, carry):
        behind, here = carry
        following = half_ref[k, first + i + 1]
        ahead = bent(here - following)
        store(i, settled(here, behind, ahead))
        return ahead, following

    lax.fori_loop(0, count, body, (bent(before - here), here), unroll=2)


def inner_columns(half_ref, part_ref, fresh_ref, first):
    for k in range(2):

        def store(i, column):
            fresh_ref[k, i] = column
            part_ref[k, i] = column.astype(BF16)

        run_of_columns(half_ref, k, first, part_ref.shape[1], store)


def gradient_kernel(groups, pieces, final, *refs):
    weight_refs = refs[:groups]
    window_refs = refs[groups : 2 * groups]
    volume_ref, half_ref = refs[2 * groups : 2 * groups + 2]
    _, share, depth, rows = half_ref.shape
    views, cols, _ = weight_refs[0].shape
    chunk = share // pieces
    span = chunk * depth
    windows = [
        jnp.concatenate(
            [jnp.concatenate([ref[v, 0], ref[v, 1]], axis=1) for v in range(views)], axis=0
        )
        for ref in window_refs
    ]
    for i in range(pieces):
        gradient = None
        for g in range(groups):
            product = lax.dot_general(
                weight_refs[g][:, :, i * span : (i + 1) * span].reshape(views * cols, span),
                windows[g],
                (((0,), (0,)), ((), ())),
                preferred_element_type=F32,
            )
            gradient = product if gradient is None else gradient + product
        for k in range(2):
            plane = gradient[:, k * rows : (k + 1) * rows].reshape(chunk, depth, rows)
            held = slice(i * chunk, (i + 1) * chunk)
            half_ref[k, held] = volume_ref[k, held] - step_size * plane
    if final:
        low_ref, high_ref, part_ref, fresh_ref = refs[2 * groups + 2 :]
        low_ref[...] = half_ref[:, :1].astype(BF16)
        high_ref[...] = half_ref[:, share - 1 :].astype(BF16)
        inner_columns(half_ref, part_ref, fresh_ref, inner_runs(share)[0][0])


def half_step_of(weights, windows, volume, final):
    groups = len(windows)
    _, share, depth, rows = volume.shape
    vmem = pl.BlockSpec(memory_space=VMEM)
    edge = VMEM((2, 1, depth, rows), BF16)
    inner = (2, inner_runs(share)[0][1], depth, rows)
    outs = (VMEM((2, share, depth, rows), F32),)
    if final:
        outs += (edge, edge, VMEM(inner, BF16), VMEM(inner, F32))
    return pl.pallas_call(
        functools.partial(gradient_kernel, groups, min(4, share), final),
        out_shape=outs,
        in_specs=[vmem] * (2 * groups + 1),
        out_specs=(vmem,) * len(outs),
        compiler_params=limit(20),
        name="half_step",
    )(*near(*weights, *windows, volume))


def second_kernel(half_ref, part_ref, fresh_ref):
    inner_columns(half_ref, part_ref, fresh_ref, inner_runs(half_ref.shape[1])[1][0])


def second_part(half):
    _, share, depth, rows = half.shape
    vmem = pl.BlockSpec(memory_space=VMEM)
    inner = (2, inner_runs(share)[1][1], depth, rows)
    return pl.pallas_call(
        second_kernel,
        out_shape=(VMEM(inner, BF16), VMEM(inner, F32)),
        in_specs=[vmem],
        out_specs=(vmem, vmem),
        compiler_params=limit(16),
        name="second_part",
    )(*near(half))


def third_kernel(half_ref, before_ref, after_ref, first_ref, second_ref, part_ref, whole_ref, *rest):
    edges, sems = rest
    share = half_ref.shape[1]
    start = share_at(0, whole_ref.shape[1] // share) * share
    puts = []

    def put(source, target, count):
        puts.append(
            pltpu.make_async_copy(
                source, whole_ref.at[:, pl.ds(start + target, count)], sems.at[len(puts)]
            )
        )
        puts[-1].start()

    for ref, run in zip((first_ref, second_ref), inner_runs(share)):
        put(ref, *run)
    for k in range(2):
        for n, (c, before, after) in enumerate(
            (
                (0, before_ref[k, 0].astype(F32), half_ref[k, 1]),
                (share - 1, half_ref[k, share - 2], after_ref[k, 0].astype(F32)),
            )
        ):
            here = half_ref[k, c]
            column = settled(here, bent(before - here), bent(here - after))
            edges[k, n] = column
            part_ref[k, n] = column.astype(BF16)
    put(edges.at[:, pl.ds(0, 1)], 0, 1)
    put(edges.at[:, pl.ds(1, 1)], share - 1, 1)
    for move in puts:
        move.wait()


def third_part(half, before, after, first, second, vcols):
    _, _, depth, rows = half.shape
    vmem = pl.BlockSpec(memory_space=VMEM)
    return pl.pallas_call(
        third_kernel,
        out_shape=(
            VMEM((2, 2, depth, rows), BF16),
            jax.ShapeDtypeStruct((2, vcols, depth, rows), F32),
        ),
        in_specs=[vmem] * 5,
        out_specs=(vmem, pl.BlockSpec(memory_space=pl.ANY)),
        scratch_shapes=[VMEM((2, 2, depth, rows), F32), pltpu.SemaphoreType.DMA((4,))],
        compiler_params=limit(16),
        name="third_part",
    )(*near(half, before, after, first, second))


def place_kernel(kinds, groups, *refs):
    count = len(kinds)
    parts, whole_ref, fresh, sems = refs[:count], refs[count + 1], refs[count + 2 : -1], refs[-1]
    share = whole_ref.shape[1] // groups
    puts = []
    for n, ((kind, j), ref) in enumerate(zip(kinds, parts)):
        first = share_at(j, groups) * share
        runs = ((0, 0, 1), (1, share - 1, 1)) if kind == 2 else ((0, *inner_runs(share)[kind]),)
        for place, (source, target, count) in enumerate(runs):
            for k in range(2):
                fresh[n][k, source : source + count] = ref[k, source : source + count].astype(F32)
                puts.append(
                    pltpu.make_async_copy(
                        fresh[n].at[k, pl.ds(source, count)],
                        whole_ref.at[k, pl.ds(first + target, count)],
                        sems.at[n, k, place],
                    )
                )
                puts[-1].start()
    for put in puts:
        put.wait()


def place(kinds, parts, whole, groups):
    hbm = pl.BlockSpec(memory_space=pl.ANY)
    vmem = pl.BlockSpec(memory_space=VMEM)
    return pl.pallas_call(
        functools.partial(place_kernel, kinds, groups),
        out_shape=jax.ShapeDtypeStruct(whole.shape, F32),
        in_specs=[vmem] * len(parts) + [hbm],
        out_specs=hbm,
        scratch_shapes=[VMEM(part.shape, F32) for part in parts]
        + [pltpu.SemaphoreType.DMA((len(parts), 2, 2))],
        input_output_aliases={len(parts): 0},
        compiler_params=limit(16),
        name="place",
    )(*near(*parts), whole)


def per_device(
    object_band,
    dual_band,
    probe_field,
    positions,
    live_counts,
    photon_counts,
    footprints,
    weights,
    volume,
):
    tiles, groups = lax.axis_size("tile"), lax.axis_size("view")
    tile_cols = object_band.shape[2]
    foot_cols = weights.shape[1]
    footprints = footprints[:, 0]
    forward = dft_block(probe_field.shape[1], False)
    inverse = dft_block(probe_field.shape[1], True)

    view_masks = masks_of(groups)
    later = [j for j in range(groups) if j not in view_masks]
    object_low = object_band.astype(BF16)
    early_shares = deal(weights, groups, view_masks)
    late_shares = deal(weights, groups, later)
    dealt = dict(zip(view_masks + later, early_shares + late_shares))
    dealt = [dealt[j] for j in range(groups)]
    weight_pieces = [dealt[0]]
    for j in range(1, groups):
        weight_pieces.append(swapped(dealt[j], "view", j))
    keep, send, volume_own = project(footprints, dealt, volume, tiles, tile_cols)
    ahead_one = passed_along(object_low, "tile", -1)
    ahead_two = passed_along(object_low, "tile", -2)
    token = None
    for mask in [1] + masks_of(tiles)[:0:-1]:
        arrived = swapped(send, "tile", mask)
        if keep.shape[0] > 1:
            keep, send = fold(keep, arrived)
            token = send if token is None else token
    projection = keep[0] + arrived[0].astype(F32)

    own_update, spill_one, spill_two = patches(
        positions,
        live_counts[:, 0],
        object_band,
        ahead_one,
        ahead_two,
        probe_field,
        forward,
        inverse,
        photon_counts,
        token,
    )
    from_one = passed_along(spill_one, "tile", 1)
    from_two = passed_along(spill_two, "tile", 2)
    summed = own_update + from_one.astype(F32) + from_two.astype(F32)
    object_new = (
        object_band
        + summed[:, 0:2] / (1.0 + summed[:, 2:3])
        - rho_weight * (object_band - projection - dual_band)
    )
    dual_new = dual_band + projection - object_new
    residual = (projection - object_new + dual_band).astype(BF16)

    pieces = [residual]
    for n in range(1, tiles // 2):
        pieces.append(swapped(residual, "tile", 2 * n))
    others = swapped(jnp.stack(pieces), "tile", 1)
    windows = cut(footprints, [piece[None] for piece in pieces] + [others], foot_cols, tiles)
    all_windows = [windows]
    for j in window_order(groups):
        all_windows.append(swapped(windows, "view", j))
    weight_pieces = [weight_pieces[j] for j in [0] + window_order(groups)]

    middle = groups // 2
    (half,) = half_step_of(weight_pieces[:middle], all_windows[:middle], volume_own, False)
    half, low_edge, high_edge, part_a, fresh_a = half_step_of(
        weight_pieces[middle:], all_windows[middle:], half, True
    )
    order = []
    for t in range(tiles):
        order += [gray(r) * tiles + t for r in range(groups)][:: -1 if t % 2 else 1]
    up = list(zip(order[:-1], order[1:]))
    before = lax.ppermute(high_edge, ("view", "tile"), up)
    after = lax.ppermute(low_edge, ("view", "tile"), [(b, a) for a, b in up])
    part_b, fresh_b = second_part(half)
    part_c, volume_new = third_part(half, before, after, fresh_a, fresh_b, volume.shape[1])
    held = {(0, 0): part_a, (1, 0): part_b, (2, 0): part_c}
    for masks in zip(view_masks, view_masks[::-1], view_masks):
        arrived = {}
        for (kind, j), value in held.items():
            arrived[kind, j ^ masks[kind]] = swapped(value, "view", masks[kind])
        held.update(arrived)
    rounds = [[(kind, mask) for mask in view_masks] for kind in range(3)]
    far_keys = [j for j in range(1, groups) if j not in view_masks]
    rounds += [[(0, j)] for j in far_keys] + [[(2, j), (1, j)] for j in far_keys]
    for keys in rounds:
        volume_new = place(keys, [held[key] for key in keys], volume_new, groups)
    return (object_new, dual_new, volume_new)


def solution(mesh):
    return jax.shard_map(
        per_device,
        mesh=mesh,
        in_specs=(
            P("view", None, "tile", None),
            P("view", None, "tile", None),
            P(),
            P("view", "tile"),
            P("view", "tile"),
            P("view", "tile", None, None),
            P("view", "tile"),
            P("view", None, "tile"),
            P(None, "tile", None, None),
        ),
        out_specs=(
            P("view", None, "tile", None),
            P("view", None, "tile", None),
            P(None, "tile", None, None),
        ),
        check_vma=False,
    )
```

```python
import functools
import numpy as np
import jax
import jax.numpy as jnp
from jax import lax
from jax.experimental import pallas as pl
from jax.experimental.pallas import tpu as pltpu
from jax.sharding import PartitionSpec as P


rho_weight = 0.5
step_size = 0.5
prior_weight = 0.5
floor_term = 0.25


F32 = jnp.float32
BF16 = jnp.bfloat16
VMEM = pltpu.VMEM
SMEM = pltpu.SMEM


def passed_along(value, axis, steps):
    count = lax.axis_size(axis)
    initial, last = (max(0, -steps), min(count, count - steps))
    return lax.ppermute(value, axis, [(source, source + steps) for source in range(initial, last)])


def near(*arrays):
    return tuple(pltpu.with_memory_space_constraint(array, VMEM) for array in arrays)


def far(*arrays):
    return tuple(pltpu.with_memory_space_constraint(array, pltpu.HBM) for array in arrays)


def limit(mebibytes):
    return pltpu.CompilerParams(vmem_limit_bytes=mebibytes << 20)


def window_order(groups):
    masks = masks_of(groups)
    return masks[-1:] + [j for j in range(1, groups) if j not in masks] + masks[:-1]


def swapped(value, axis, mask):
    count = lax.axis_size(axis)
    return lax.ppermute(value, axis, [(i, i ^ mask) for i in range(count)])


def masks_of(count):
    return [1 << b for b in range(count.bit_length() - 1)]


def gray(rank):
    return rank ^ (rank >> 1)


def share_at(j, groups):
    rank = lax.axis_index("view") ^ j
    shift = 1
    while shift < groups:
        rank = rank ^ (rank >> shift)
        shift *= 2
    return jnp.where((lax.axis_index("tile") & 1) == 1, groups - 1 - rank, rank)


def dft_block(order_n, inverse):
    counter = np.arange(order_n)
    angles = (counter[:, None] * counter[None, :] % order_n) * (2.0 * np.pi / order_n)
    re = np.cos(angles) / np.sqrt(order_n)
    im = -np.sin(angles) / np.sqrt(order_n)
    im = -im if inverse else im
    return jnp.asarray(np.block([[re, -im], [im, re]]).astype(np.float32)).astype(BF16)


def deal_kernel(groups, offsets, weights_ref, *refs):
    *shares, sems = refs
    copies = []
    for n, (j, ref) in enumerate(zip(offsets, shares)):
        size = ref.shape[2]
        first = pl.multiple_of(share_at(j, groups) * size, size)
        copies.append(
            pltpu.make_async_copy(weights_ref.at[:, :, pl.ds(first, size)], ref, sems.at[n])
        )
        copies[-1].start()
    for copy in copies:
        copy.wait()


def deal(weights, groups, offsets):
    views, cols, voxels = weights.shape
    vmem = pl.BlockSpec(memory_space=VMEM)
    return pl.pallas_call(
        functools.partial(deal_kernel, groups, offsets),
        out_shape=(VMEM((views, cols, voxels // groups), BF16),) * len(offsets),
        in_specs=[pl.BlockSpec(memory_space=pl.ANY)],
        out_specs=(vmem,) * len(offsets),
        scratch_shapes=[pltpu.SemaphoreType.DMA((len(offsets),))],
        compiler_params=limit(8),
        name="deal",
    )(*far(weights))


def ranks(footprints, views, parts, tiles):
    tile = lax.axis_index("tile")
    found = []
    for v in range(views):
        row = []
        for part in range(parts):
            other = (footprints[v] + part) ^ tile
            row.append((other >> 1) + (other & 1) * (tiles // 2))
        found.append(row)
    return found


def project_kernel(pieces, footprints_ref, volume_ref, *refs):
    *shares, keep_ref, send_ref, part_ref, footprints, sem = refs
    groups = len(shares)
    views, cols, _ = shares[0].shape
    _, count, depth, rows = part_ref.shape
    half, _, _, width, _ = keep_ref.shape
    chunk = count // pieces
    span = chunk * depth
    spots_copy = pltpu.make_async_copy(footprints_ref, footprints, sem)
    spots_copy.start()
    keep_ref[...] = jnp.zeros_like(keep_ref)
    send_ref[...] = jnp.zeros_like(send_ref)
    total = jnp.zeros((views * cols, 2 * rows), F32)
    for j, ref in enumerate(shares):
        at = share_at(j, groups) * count
        for i in range(pieces):
            low = jnp.concatenate(
                [
                    volume_ref[k, pl.ds(at + i * chunk, chunk)].reshape(span, rows).astype(BF16)
                    for k in range(2)
                ],
                axis=1,
            )
            total = total + jnp.dot(
                ref[:, :, i * span : (i + 1) * span].reshape(views * cols, span),
                low,
                preferred_element_type=F32,
            )
        if j == 0:
            part_ref[...] = volume_ref[:, pl.ds(at, count)]
    spots_copy.wait()
    spots = ranks(footprints, views, cols // width, 2 * half)
    for v in range(views):
        for part in range(cols // width):
            first = v * cols + part * width
            spot = spots[v][part]
            for ref, wanted, index in (
                (keep_ref, spot < half, spot),
                (send_ref, spot >= half, spot - half),
            ):

                @pl.when(wanted)
                def _():
                    for k in range(2):
                        ref[index, v, k] = total[
                            first : first + width, k * rows : (k + 1) * rows
                        ].astype(BF16)


def project(footprints, shares, volume, tiles, tile_cols):
    groups = len(shares)
    views, _, _ = shares[0].shape
    _, vcols, depth, rows = volume.shape
    count = vcols // groups
    pieces = 2 if count % 2 == 0 else 1
    vmem = pl.BlockSpec(memory_space=VMEM)
    hbm = pl.BlockSpec(memory_space=pl.ANY)
    placed = VMEM((tiles // 2, views, 2, tile_cols, rows), BF16)
    return pl.pallas_call(
        functools.partial(project_kernel, pieces),
        out_shape=(placed, placed, VMEM((2, count, depth, rows), F32)),
        in_specs=[hbm, vmem] + [vmem] * groups,
        out_specs=(vmem,) * 3,
        scratch_shapes=[
            SMEM(footprints.shape, jnp.int32),
            pltpu.SemaphoreType.DMA(()),
        ],
        compiler_params=limit(20),
        name="project",
    )(*far(footprints), volume, *near(*shares))


def fold_kernel(keep_ref, arrived_ref, near_ref, send_ref):
    half = near_ref.shape[0]
    near_ref[...] = keep_ref[:half].astype(F32) + arrived_ref[:half].astype(F32)
    send_ref[...] = (keep_ref[half:].astype(F32) + arrived_ref[half:].astype(F32)).astype(BF16)


def fold(keep, arrived):
    vmem = pl.BlockSpec(memory_space=VMEM)
    shape = (keep.shape[0] // 2,) + keep.shape[1:]
    return pl.pallas_call(
        fold_kernel,
        out_shape=(VMEM(shape, F32), VMEM(shape, BF16)),
        in_specs=[vmem] * 2,
        out_specs=(vmem,) * 2,
        compiler_params=limit(8),
        name="fold",
    )(*near(keep, arrived))


GROUP = 8


def patch_kernel(
    positions,
    live,
    own_ref,
    one_ref,
    two_ref,
    probe_ref,
    forward_ref,
    inverse_ref,
    counts_ref,
    token_ref,
    near_ref,
    ahead_one_ref,
    ahead_two_ref,
    reach,
    total,
    buffer,
    sems,
):
    views, _, width, rows = own_ref.shape
    cols = probe_ref.shape[1]
    span = 3 * width
    for part, ref in enumerate((own_ref, one_ref, two_ref)):
        reach[:, :, part * width : (part + 1) * width, :] = ref[...].astype(F32)
    total[...] = jnp.zeros_like(total)
    starts = [0]
    for v in range(views):
        starts.append(starts[-1] + lax.div(live[v] + (GROUP - 1), GROUP))

    def located(step):
        view, first = 0, 0
        for v in range(1, views):
            after = (step >= starts[v]).astype(jnp.int32)
            view = view + after
            first = jnp.where(after == 1, starts[v], first)
        return view, (step - first) * GROUP

    def fetch(step, slot):
        view, first = located(step)
        return pltpu.make_async_copy(
            counts_ref.at[view, pl.ds(first, GROUP)], buffer.at[slot], sems.at[slot]
        )

    fetch(0, 0).start()

    def body(step, carry):
        slot = step & 1
        view, first = located(step)
        pltpu.make_async_copy(
            counts_ref.at[view, pl.ds(first, GROUP)], buffer.at[slot], sems.at[slot]
        ).wait()

        @pl.when(step + 1 < starts[views])
        def _():
            fetch(step + 1, 1 - slot).start()

        probe_re = probe_ref[0]
        probe_im = probe_ref[1]
        spots = []
        exits = []
        for g in range(GROUP):
            offset = positions[view, first + g]
            spots.append(jnp.where(first + g < live[view], offset, span))
            obj_re = reach[view, 0, pl.ds(offset, cols), :]
            obj_im = reach[view, 1, pl.ds(offset, cols), :]
            wave_re = (probe_re * obj_re - probe_im * obj_im).astype(BF16)
            wave_im = (probe_re * obj_im + probe_im * obj_re).astype(BF16)
            exits.append(jnp.concatenate([wave_re, wave_im], axis=0))
        waves = jnp.concatenate(exits, axis=1)
        done = jnp.dot(forward_ref[...], waves, preferred_element_type=F32).astype(BF16)
        done = jnp.concatenate(
            [
                jnp.concatenate(
                    [
                        done[:cols, g * rows : (g + 1) * rows],
                        done[cols:, g * rows : (g + 1) * rows],
                    ],
                    axis=1,
                )
                for g in range(GROUP)
            ],
            axis=0,
        )
        spectrum = jnp.dot(done, inverse_ref[...], preferred_element_type=F32)
        spec_re = spectrum[:, :rows]
        spec_im = spectrum[:, rows:]
        counts = buffer[slot].reshape(GROUP * cols, rows).astype(F32)
        square = spec_re * spec_re + spec_im * spec_im + floor_term
        factor = (counts * (1.0 / 16.0)) * lax.rsqrt(jnp.maximum(counts * square, 1e-6))
        replaced = jnp.concatenate(
            [(spec_re * factor).astype(BF16), (spec_im * factor).astype(BF16)], axis=1
        )
        back = jnp.dot(replaced, forward_ref[...], preferred_element_type=F32).astype(BF16)
        back = jnp.concatenate(
            [
                jnp.concatenate(
                    [
                        back[g * cols : (g + 1) * cols, :rows],
                        back[g * cols : (g + 1) * cols, rows:],
                    ],
                    axis=0,
                )
                for g in range(GROUP)
            ],
            axis=1,
        )
        wave = jnp.dot(inverse_ref[...], back, preferred_element_type=F32)
        power = probe_re * probe_re + probe_im * probe_im
        for g in range(GROUP):
            diff = wave[:, g * rows : (g + 1) * rows] - exits[g].astype(F32)
            diff_re = diff[:cols]
            diff_im = diff[cols:]
            place = pl.ds(spots[g], cols)
            total[view, 0, place, :] += probe_re * diff_re + probe_im * diff_im
            total[view, 1, place, :] += probe_re * diff_im - probe_im * diff_re
            total[view, 2, place, :] += power
        return carry

    lax.fori_loop(0, starts[views], body, 0)
    near_ref[...] = total[:, :, :width, :]
    for part, ref in ((1, ahead_one_ref), (2, ahead_two_ref)):
        ref[...] = total[:, :, part * width : (part + 1) * width, :].astype(BF16)


def patches(positions, live, own, one, two, probe, forward, inverse, counts, token):
    views, _, width, rows = own.shape
    cols = probe.shape[1]
    slots = counts.shape[1]
    vmem = pl.BlockSpec(memory_space=VMEM)
    smem = pl.BlockSpec(memory_space=SMEM)
    return pl.pallas_call(
        patch_kernel,
        out_shape=(
            VMEM((views, 3, width, rows), F32),
            VMEM((views, 3, width, rows), BF16),
            VMEM((views, 3, width, rows), BF16),
        ),
        in_specs=[smem, smem] + [vmem] * 6 + [pl.BlockSpec(memory_space=pl.ANY)] * 2,
        out_specs=(vmem, vmem, vmem),
        scratch_shapes=[
            VMEM((views, 2, 3 * width, rows), F32),
            VMEM((views, 3, 3 * width + cols, rows), F32),
            VMEM((2, GROUP, cols, rows), jnp.int32),
            pltpu.SemaphoreType.DMA((2,)),
        ],
        compiler_params=limit(20),
        cost_estimate=pl.CostEstimate(
            flops=views * slots * 16 * cols * cols * rows,
            transcendentals=0,
            bytes_accessed=counts.size * 4,
        ),
        name="patches",
    )(positions, live, own, *near(one, two), probe, forward, inverse, counts, *near(token))


def cut_kernel(tiles, footprints, *refs):
    pieces, windows_ref = refs[:-1], refs[-1]
    views, _, cols, _ = windows_ref.shape
    width = pieces[0].shape[3]
    spots = ranks(footprints, views, cols // width, tiles)
    for v in range(views):
        for part in range(cols // width):
            first = 0
            for ref in pieces:
                inside = spots[v][part] - first

                @pl.when((inside >= 0) & (inside < ref.shape[0]))
                def _():
                    windows_ref[v, :, part * width : (part + 1) * width] = ref[inside, v]

                first += ref.shape[0]


def cut(footprints, pieces, cols, tiles):
    _, views, planes, _, rows = pieces[0].shape
    vmem = pl.BlockSpec(memory_space=VMEM)
    return pl.pallas_call(
        functools.partial(cut_kernel, tiles),
        out_shape=VMEM((views, planes, cols, rows), BF16),
        in_specs=[pl.BlockSpec(memory_space=SMEM)] + [vmem] * len(pieces),
        out_specs=vmem,
        compiler_params=limit(8),
        name="cut",
    )(footprints, *near(*pieces))


def inner_runs(share):
    first = max(1, share // 2 - 2)
    return ((1, first), (1 + first, share - 2 - first))


def bent(d):
    return d * lax.rsqrt(1.0 + d * d)


def settled(here, behind, ahead):
    depth, rows = here.shape
    lane = lax.broadcasted_iota(jnp.int32, (depth, rows), 1)
    level = lax.broadcasted_iota(jnp.int32, (depth, rows), 0)
    prior = ahead - behind
    beyond = jnp.where(lane == rows - 1, 0.0, pltpu.roll(here, rows - 1, 1))
    pair = bent(here - beyond)
    prior = prior + pair - jnp.where(lane == 0, -bent(here), pltpu.roll(pair, 1, 1))
    beyond = jnp.where(level == depth - 1, 0.0, pltpu.roll(here, depth - 1, 0))
    pair = bent(here - beyond)
    prior = prior + pair - jnp.where(level == 0, -bent(here[:1]), pltpu.roll(pair, 1, 0))
    return here - step_size * prior_weight * prior


def run_of_columns(half_ref, k, first, count, store):
    before = half_ref[k, first - 1]
    here = half_ref[k, first]

    def body(i, carry):
        behind, here = carry
        following = half_ref[k, first + i + 1]
        ahead = bent(here - following)
        store(i, settled(here, behind, ahead))
        return ahead, following

    lax.fori_loop(0, count, body, (bent(before - here), here), unroll=2)


def inner_columns(half_ref, part_ref, fresh_ref, first):
    for k in range(2):

        def store(i, column):
            fresh_ref[k, i] = column
            part_ref[k, i] = column.astype(BF16)

        run_of_columns(half_ref, k, first, part_ref.shape[1], store)


def gradient_kernel(groups, pieces, final, *refs):
    weight_refs = refs[:groups]
    window_refs = refs[groups : 2 * groups]
    volume_ref, half_ref = refs[2 * groups : 2 * groups + 2]
    _, share, depth, rows = half_ref.shape
    views, cols, _ = weight_refs[0].shape
    chunk = share // pieces
    span = chunk * depth
    windows = [
        jnp.concatenate(
            [jnp.concatenate([ref[v, 0], ref[v, 1]], axis=1) for v in range(views)], axis=0
        )
        for ref in window_refs
    ]
    for i in range(pieces):
        gradient = None
        for g in range(groups):
            product = lax.dot_general(
                weight_refs[g][:, :, i * span : (i + 1) * span].reshape(views * cols, span),
                windows[g],
                (((0,), (0,)), ((), ())),
                preferred_element_type=F32,
            )
            gradient = product if gradient is None else gradient + product
        for k in range(2):
            plane = gradient[:, k * rows : (k + 1) * rows].reshape(chunk, depth, rows)
            held = slice(i * chunk, (i + 1) * chunk)
            half_ref[k, held] = volume_ref[k, held] - step_size * plane
    if final:
        low_ref, high_ref, part_ref, fresh_ref = refs[2 * groups + 2 :]
        low, high = half_ref[:, :1].astype(F32), half_ref[:, share - 1 :].astype(F32)
        odd = share_at(0, lax.axis_size("view")) & 1
        low_ref[...] = jnp.where(odd == 1, low, high).astype(BF16)
        high_ref[...] = jnp.where(odd == 1, high, low).astype(BF16)
        inner_columns(half_ref, part_ref, fresh_ref, inner_runs(share)[0][0])


def half_step_of(weights, windows, volume, final):
    groups = len(windows)
    _, share, depth, rows = volume.shape
    vmem = pl.BlockSpec(memory_space=VMEM)
    edge = VMEM((2, 1, depth, rows), BF16)
    inner = (2, inner_runs(share)[0][1], depth, rows)
    outs = (VMEM((2, share, depth, rows), F32),)
    if final:
        outs += (edge, edge, VMEM(inner, BF16), VMEM(inner, F32))
    return pl.pallas_call(
        functools.partial(gradient_kernel, groups, min(4, share), final),
        out_shape=outs,
        in_specs=[vmem] * (2 * groups + 1),
        out_specs=(vmem,) * len(outs),
        compiler_params=limit(20),
        name="half_step",
    )(*near(*weights, *windows, volume))


def second_kernel(half_ref, part_ref, fresh_ref):
    inner_columns(half_ref, part_ref, fresh_ref, inner_runs(half_ref.shape[1])[1][0])


def second_part(half):
    _, share, depth, rows = half.shape
    vmem = pl.BlockSpec(memory_space=VMEM)
    inner = (2, inner_runs(share)[1][1], depth, rows)
    return pl.pallas_call(
        second_kernel,
        out_shape=(VMEM(inner, BF16), VMEM(inner, F32)),
        in_specs=[vmem],
        out_specs=(vmem, vmem),
        compiler_params=limit(16),
        name="second_part",
    )(*near(half))


def third_kernel(half_ref, inside_ref, across_ref, first_ref, second_ref, part_ref, whole_ref, *rest):
    edges, sems = rest
    share = half_ref.shape[1]
    start = share_at(0, whole_ref.shape[1] // share) * share
    puts = []

    def put(source, target, count):
        puts.append(
            pltpu.make_async_copy(
                source, whole_ref.at[:, pl.ds(start + target, count)], sems.at[len(puts)]
            )
        )
        puts[-1].start()

    for ref, run in zip((first_ref, second_ref), inner_runs(share)):
        put(ref, *run)
    odd = share_at(0, whole_ref.shape[1] // share) & 1
    for k in range(2):
        inside, across = inside_ref[k, 0].astype(F32), across_ref[k, 0].astype(F32)
        for n, (c, before, after) in enumerate(
            (
                (0, jnp.where(odd == 1, inside, across), half_ref[k, 1]),
                (share - 1, half_ref[k, share - 2], jnp.where(odd == 1, across, inside)),
            )
        ):
            here = half_ref[k, c]
            column = settled(here, bent(before - here), bent(here - after))
            edges[k, n] = column
            part_ref[k, n] = column.astype(BF16)
    put(edges.at[:, pl.ds(0, 1)], 0, 1)
    put(edges.at[:, pl.ds(1, 1)], share - 1, 1)
    for move in puts:
        move.wait()


def third_part(half, inside, across, first, second, vcols):
    _, _, depth, rows = half.shape
    vmem = pl.BlockSpec(memory_space=VMEM)
    return pl.pallas_call(
        third_kernel,
        out_shape=(
            VMEM((2, 2, depth, rows), BF16),
            jax.ShapeDtypeStruct((2, vcols, depth, rows), F32),
        ),
        in_specs=[vmem] * 5,
        out_specs=(vmem, pl.BlockSpec(memory_space=pl.ANY)),
        scratch_shapes=[VMEM((2, 2, depth, rows), F32), pltpu.SemaphoreType.DMA((4,))],
        compiler_params=limit(16),
        name="third_part",
    )(*near(half, inside, across, first, second))


def place_kernel(kinds, groups, *refs):
    count = len(kinds)
    parts, whole_ref, fresh, sems = refs[:count], refs[count + 1], refs[count + 2 : -1], refs[-1]
    share = whole_ref.shape[1] // groups
    puts = []
    for n, ((kind, j), ref) in enumerate(zip(kinds, parts)):
        first = share_at(j, groups) * share
        runs = ((0, 0, 1), (1, share - 1, 1)) if kind == 2 else ((0, *inner_runs(share)[kind]),)
        for place, (source, target, count) in enumerate(runs):
            for k in range(2):
                fresh[n][k, source : source + count] = ref[k, source : source + count].astype(F32)
                puts.append(
                    pltpu.make_async_copy(
                        fresh[n].at[k, pl.ds(source, count)],
                        whole_ref.at[k, pl.ds(first + target, count)],
                        sems.at[n, k, place],
                    )
                )
                puts[-1].start()
    for put in puts:
        put.wait()


def place(kinds, parts, whole, groups):
    hbm = pl.BlockSpec(memory_space=pl.ANY)
    vmem = pl.BlockSpec(memory_space=VMEM)
    return pl.pallas_call(
        functools.partial(place_kernel, kinds, groups),
        out_shape=jax.ShapeDtypeStruct(whole.shape, F32),
        in_specs=[vmem] * len(parts) + [hbm],
        out_specs=hbm,
        scratch_shapes=[VMEM(part.shape, F32) for part in parts]
        + [pltpu.SemaphoreType.DMA((len(parts), 2, 2))],
        input_output_aliases={len(parts): 0},
        compiler_params=limit(16),
        name="place",
    )(*near(*parts), whole)


def per_device(
    object_band,
    dual_band,
    probe_field,
    positions,
    live_counts,
    photon_counts,
    footprints,
    weights,
    volume,
):
    tiles, groups = lax.axis_size("tile"), lax.axis_size("view")
    tile_cols = object_band.shape[2]
    foot_cols = weights.shape[1]
    footprints = footprints[:, 0]
    forward = dft_block(probe_field.shape[1], False)
    inverse = dft_block(probe_field.shape[1], True)

    view_masks = masks_of(groups)
    later = [j for j in range(groups) if j not in view_masks]
    object_low = object_band.astype(BF16)
    early_shares = deal(weights, groups, view_masks)
    late_shares = deal(weights, groups, later)
    dealt = dict(zip(view_masks + later, early_shares + late_shares))
    dealt = [dealt[j] for j in range(groups)]
    weight_pieces = [dealt[0]]
    for j in range(1, groups):
        weight_pieces.append(swapped(dealt[j], "view", j))
    keep, send, volume_own = project(footprints, dealt, volume, tiles, tile_cols)
    ahead_one = passed_along(object_low, "tile", -1)
    ahead_two = passed_along(object_low, "tile", -2)
    token = None
    for mask in [1] + masks_of(tiles)[:0:-1]:
        arrived = swapped(send, "tile", mask)
        if keep.shape[0] > 1:
            keep, send = fold(keep, arrived)
            token = send if token is None else token
    projection = keep[0] + arrived[0].astype(F32)

    own_update, spill_one, spill_two = patches(
        positions,
        live_counts[:, 0],
        object_band,
        ahead_one,
        ahead_two,
        probe_field,
        forward,
        inverse,
        photon_counts,
        token,
    )
    from_one = passed_along(spill_one, "tile", 1)
    from_two = passed_along(spill_two, "tile", 2)
    summed = own_update + from_one.astype(F32) + from_two.astype(F32)
    object_new = (
        object_band
        + summed[:, 0:2] / (1.0 + summed[:, 2:3])
        - rho_weight * (object_band - projection - dual_band)
    )
    dual_new = dual_band + projection - object_new
    residual = (projection - object_new + dual_band).astype(BF16)

    pieces = [residual]
    for n in range(1, tiles // 2):
        pieces.append(swapped(residual, "tile", 2 * n))
    others = swapped(jnp.stack(pieces), "tile", 1)
    windows = cut(footprints, [piece[None] for piece in pieces] + [others], foot_cols, tiles)
    all_windows = [windows]
    for j in window_order(groups):
        all_windows.append(swapped(windows, "view", j))
    weight_pieces = [weight_pieces[j] for j in [0] + window_order(groups)]

    middle = groups // 2
    (half,) = half_step_of(weight_pieces[:middle], all_windows[:middle], volume_own, False)
    half, inner_edge, outer_edge, part_a, fresh_a = half_step_of(
        weight_pieces[middle:], all_windows[middle:], half, True
    )
    order = []
    for t in range(tiles):
        order += [gray(r) * tiles + t for r in range(groups)][:: -1 if t % 2 else 1]
    links = list(zip(order[:-1], order[1:]))
    links = [links[start::2] + [(b, a) for a, b in links[start::2]] for start in range(2)]
    inside = lax.ppermute(inner_edge, ("view", "tile"), links[0])
    across = lax.ppermute(outer_edge, ("view", "tile"), links[1])
    part_b, fresh_b = second_part(half)
    part_c, volume_new = third_part(half, inside, across, fresh_a, fresh_b, volume.shape[1])
    held = {(0, 0): part_a, (1, 0): part_b, (2, 0): part_c}
    for masks in zip(view_masks, view_masks[::-1], view_masks):
        arrived = {}
        for (kind, j), value in held.items():
            arrived[kind, j ^ masks[kind]] = swapped(value, "view", masks[kind])
        held.update(arrived)
    rounds = [[(kind, mask) for mask in view_masks] for kind in range(3)]
    far_keys = [j for j in range(1, groups) if j not in view_masks]
    rounds += [[(0, j)] for j in far_keys] + [[(2, j), (1, j)] for j in far_keys]
    for keys in rounds:
        volume_new = place(keys, [held[key] for key in keys], volume_new, groups)
    return (object_new, dual_new, volume_new)


def solution(mesh):
    return jax.shard_map(
        per_device,
        mesh=mesh,
        in_specs=(
            P("view", None, "tile", None),
            P("view", None, "tile", None),
            P(),
            P("view", "tile"),
            P("view", "tile"),
            P("view", "tile", None, None),
            P("view", "tile"),
            P("view", None, "tile"),
            P(None, "tile", None, None),
        ),
        out_specs=(
            P("view", None, "tile", None),
            P("view", None, "tile", None),
            P(None, "tile", None, None),
        ),
        check_vma=False,
    )
```
